512 devices in a mesh: src: 64 (over z_hi, x, y), tile: 8 (over z_lo, core).
Axes of the slice: x: 4, y: 4, z: 16 (z_hi: 4, z_lo: 4; z = z_hi * 4 + z_lo), core: 2. Of those that a mesh axis runs over, the one named last changes fastest.
Arguments:
- target: bfloat16 [128, 512, 256], P('src', 'tile'), may hold values from -6 to 6
- sources: bfloat16 [4096, 256], P('src'), may hold values from -6 to 6
- kernel_one: bfloat16 [6, 6, 1, 16], replicated, may hold values from -1 to 1
- first_conv_bias: float32 [16], replicated, may hold values from -3 to 3
- kernel_two: bfloat16 [6, 6, 16, 32], replicated, may hold values from -0.25 to 0.25
- shift_two: float32 [32], replicated, may hold values from -3 to 3
- kernel_three: bfloat16 [6, 6, 32, 64], replicated, may hold values from -0.1875 to 0.1875
- shift_three: float32 [64], replicated, may hold values from -3 to 3
- latents: float32 [8, 128], replicated, may hold values from -6 to 6
- pos_key: float32 [16, 64, 128], P(None, 'tile'), may hold values from -6 to 6
- w_key: float32 [64, 128], replicated, may hold values from -0.5 to 0.5
- value_weight: float32 [64, 128], replicated, may hold values from -0.75 to 0.75
Outputs:
- tokens: float32 [4096, 8, 128], P('src')
The draws below stay inside these ranges and needn't reach their ends.
All inputs are finite; a program needn't handle non-finite values.
Results may differ from the reference program's by a relative error of at most 0.003.
Values may be sent and summed in bfloat16 or wider, within the bound.
No kernel may reach another device: no remote copies, remote signals or barrier semaphores. Data moves between devices by JAX's collectives and lax.ppermute only.
A program may use at most 64 MiB of HBM per device.

```python
import math
import jax
import jax.numpy as jnp
from jax import lax

C = 256
CH1 = 16
CH2 = 32
CH3 = 64
LAT = 8
DK = 128
KS = 6
S_DEV = 64
TH = 128
TWA = 512
PH = 16
PW = 64
SOURCES = 4096


def drawn_pair(key):
    latent_rows = jnp.clip(jax.random.normal(jax.random.fold_in(key, 11), (LAT, DK), jnp.float32), -4.0, 4.0)
    pos_rows = jnp.clip(jax.random.normal(jax.random.fold_in(key, 12), (PH * PW, DK), jnp.float32), -4.0, 4.0)
    return (latent_rows, pos_rows.reshape(PH, PW, DK))


def draw_latents(key, part):
    return drawn_pair(key)[0]


def draw_pos_key(key, part):
    return drawn_pair(key)[1]


def shard_levels(key, shape, split, least, top_value):
    def one(axis_at, parts):
        steps = jax.random.uniform(jax.random.fold_in(jax.random.fold_in(key, 6), axis_at), (parts,), jnp.float32, least / len(split), top_value / len(split))
        return jnp.repeat(jnp.exp(steps), shape[axis_at] // parts).reshape((-1,) + (1,) * (len(shape) - axis_at - 1))

    level = one(*split[0])
    for cut in split[1:]:
        level = level * one(*cut)
    return level


def bell_draw(rng, extent, spread, bound, pieces=(), held_as=jnp.bfloat16):
    values = spread * jax.random.normal(rng, extent, jnp.float32)
    if pieces:
        values = values * shard_levels(rng, extent, pieces, -0.22, 0.18)
    return jnp.clip(values, -bound, bound).astype(held_as)


def setup_inputs(seed: int = 0) -> dict:
    seeds = jax.random.split(jax.random.key(seed), 13)
    return {
        "target": bell_draw(seeds[0], (TH, TWA, C), 1.0, 6.0, ((0, 64), (1, 8))),
        "sources": bell_draw(seeds[1], (SOURCES, C), 1.0, 6.0, ((0, 64),)),
        "kernel_one": bell_draw(seeds[2], (KS, KS, 1, CH1), (KS * KS) ** -0.5, 1.0),
        "first_conv_bias": bell_draw(seeds[3], (CH1,), 0.5, 3.0, (), jnp.float32),
        "kernel_two": bell_draw(seeds[4], (KS, KS, CH1, CH2), (KS * KS * CH1) ** -0.5, 0.25),
        "shift_two": bell_draw(seeds[5], (CH2,), 0.5, 3.0, (), jnp.float32),
        "kernel_three": bell_draw(seeds[6], (KS, KS, CH2, CH3), (KS * KS * CH2) ** -0.5, 0.1875),
        "shift_three": bell_draw(seeds[7], (CH3,), 0.5, 3.0, (), jnp.float32),
        "latents": draw_latents(jax.random.fold_in(seeds[12], 71), 0),
        "pos_key": draw_pos_key(jax.random.fold_in(seeds[12], 71), 0),
        "w_key": bell_draw(seeds[10], (CH3, DK), DK ** -0.5, 0.5, (), jnp.float32),
        "value_weight": bell_draw(seeds[11], (CH3, DK), CH3 ** -0.5, 0.75, (), jnp.float32),
    }


highest_precision = lax.Precision.HIGHEST
conv_layout = ('NHWC', 'HWIO', 'NHWC')

def conv_layer(in_field, kernel_weights, bias_term):
    result = lax.conv_general_dilated(in_field, kernel_weights.astype(jnp.float32), (2, 2), 'VALID', dimension_numbers=conv_layout, precision=highest_precision)
    return result + bias_term

def to_half(values):
    return lax.optimization_barrier(values.astype(jnp.bfloat16)).astype(jnp.float32)

def reference(target, sources, kernel_one, first_conv_bias, kernel_two, shift_two, kernel_three, shift_three, latents, pos_key, w_key, value_weight):
    border = 7 * (kernel_one.shape[0] - 2) // 2
    corr_scale = 1.0 / math.sqrt(target.shape[2])
    key_scale = 1.0 / math.sqrt(latents.shape[1])
    padded_target = jnp.pad(target.astype(jnp.float32), ((border, border), (border, border), (0, 0)))
    query_feat = to_half(jnp.dot(latents, w_key.T, precision=highest_precision, preferred_element_type=jnp.float32))
    pos_score = jnp.einsum('ld,hwd->lhw', latents, pos_key, precision=highest_precision)

    def one_block(source_block):
        cost_map = jnp.einsum('hwc,sc->shw', padded_target, source_block.astype(jnp.float32), precision=highest_precision) * corr_scale
        cost_map = to_half(cost_map)
        hidden_one = to_half(jax.nn.gelu(conv_layer(cost_map[..., None], kernel_one, first_conv_bias)))
        hidden_two = to_half(jax.nn.gelu(conv_layer(hidden_one, kernel_two, shift_two)))
        feature_maps = to_half(conv_layer(hidden_two, kernel_three, shift_three))
        scores = (jnp.einsum('shwc,lc->slhw', feature_maps, query_feat, precision=highest_precision) + pos_score[None]) * key_scale
        peak_value = lax.optimization_barrier(jnp.max(scores, axis=(2, 3), keepdims=True))
        weights = jnp.exp(scores - peak_value)
        weights = weights / lax.optimization_barrier(jnp.sum(weights, axis=(2, 3), keepdims=True))
        attended_latents = jnp.einsum('slhw,shwc->slc', weights, feature_maps, precision=highest_precision)
        return jnp.einsum('nzk,ki->nzi', attended_latents, value_weight, precision=highest_precision)
    source_blocks = sources.reshape(-1, S_DEV, sources.shape[1])
    result = lax.map(one_block, source_blocks)
    return result.reshape(sources.shape[0], latents.shape[0], latents.shape[1])
```

```python
import functools
import math

import jax
import jax.numpy as jnp
from jax import lax
from jax.experimental import pallas as pl
from jax.experimental.pallas import tpu as pltpu
from jax.sharding import Mesh, PartitionSpec as P

exact = lax.Precision.HIGHEST
f32 = jnp.float32
bf16 = jnp.bfloat16

GROUP = 16
HALO = 16
WIDE = 96
PAIRS = 64
EDGE = 7
VMEM = 56 * 1024 * 1024


def params():
    return pltpu.CompilerParams(vmem_limit_bytes=VMEM)


def gelu(x):
    inner = x * (math.sqrt(2.0 / math.pi) + (math.sqrt(2.0 / math.pi) * 0.044715) * (x * x))
    half = 0.5 * x
    return half + half * jnp.tanh(inner)


def nt_dot(a, b):
    return lax.dot_general(a, b, (((1,), (1,)), ((), ())), preferred_element_type=f32)


def mm(a, b):
    return jnp.dot(a, b, preferred_element_type=f32)


def cost_body(rows_ref, left_ref, right_ref, sources_ref, out_ref):
    parts = []
    for z in range(rows_ref.shape[0]):
        for r in range(2):
            parts += [left_ref[z, r], rows_ref[z, r], right_ref[z, r]]
    window = jnp.concatenate(parts, axis=0)
    scale = 1.0 / math.sqrt(sources_ref.shape[-1])

    def one(i, _):
        out_ref[i] = (nt_dot(sources_ref[i], window) * scale).astype(bf16)
        return 0

    lax.fori_loop(0, sources_ref.shape[0], one, 0, unroll=4)


def cost_maps(rows, left, right, sources):
    groups, count, _ = sources.shape
    return pl.pallas_call(
        cost_body,
        out_shape=jax.ShapeDtypeStruct((groups, count, 2 * WIDE * rows.shape[0]), bf16),
        compiler_params=params(),
        name="cost_maps",
    )(rows, left, right, sources)


def band(kernel_ref, out_ref, step, block):
    _, depth, lanes = kernel_ref.shape
    rows = out_ref.shape[0] // 6
    for t in range(lanes // 128):
        lane = lax.broadcasted_iota(jnp.int32, (depth, 128), 1) // block
        for kh in range(6):
            tile = kernel_ref[kh, :, 128 * t : 128 * (t + 1)].astype(f32)
            total = jnp.zeros((rows, 128), f32)
            for b in range(128 // block):
                top = step * (b + t * (128 // block))
                piece = [jnp.where(lane == b, tile, 0.0)]
                if top:
                    piece = [jnp.zeros((top, 128), f32)] + piece
                if rows - top - depth:
                    piece = piece + [jnp.zeros((rows - top - depth, 128), f32)]
                total = total + jnp.concatenate(piece, axis=0)
            out_ref[kh * rows : (kh + 1) * rows, 128 * t : 128 * (t + 1)] = total.astype(bf16)


def band_body(one_ref, two_ref, three_ref, out_one, out_two, out_three):
    lanes = one_ref.shape[-1]
    row = lax.broadcasted_iota(jnp.int32, (WIDE, lanes), 0)
    tap = row - 2 - 2 * (lax.broadcasted_iota(jnp.int32, (WIDE, lanes), 1) // 16)
    for j in range(3):
        for q in range(2):
            total = jnp.zeros((WIDE, lanes), f32)
            for kw in range(6):
                line = one_ref[2 * j + q, kw : kw + 1, :].astype(f32)
                total = jnp.where(tap == kw, line, total)
            out_one[256 * j + WIDE * q : 256 * j + WIDE * (q + 1), :] = total.astype(bf16)
        out_one[256 * j + 2 * WIDE : 256 * (j + 1), :] = jnp.zeros((256 - 2 * WIDE, lanes), bf16)
    band(two_ref, out_two, 32, 32)
    band(three_ref, out_three, 64, 64)


def bands(kernel_one, kernel_two, kernel_three):
    one = jnp.tile(kernel_one.reshape(6, 6, 16), (1, 1, 48))
    two = jnp.tile(kernel_two.reshape(6, 96, 32), (1, 1, 8))
    three = jnp.tile(kernel_three.reshape(6, 192, 64), (1, 1, 4))
    return pl.pallas_call(
        band_body,
        out_shape=(
            jax.ShapeDtypeStruct((768, 768), bf16),
            jax.ShapeDtypeStruct((2304, 256), bf16),
            jax.ShapeDtypeStruct((2304, 256), bf16),
        ),
        compiler_params=params(),
        name="bands",
    )(one, two, three)


def encode_body(
    cost_ref,
    one_ref,
    two_ref,
    three_ref,
    bias_one,
    bias_two,
    bias_three,
    query_ref,
    pos_ref,
    spread_ref,
    out_ref,
    pairs,
    hidden_one,
    hidden_two,
    features,
    score_ref,
):
    count = cost_ref.shape[1]
    blank = jnp.zeros((EDGE, count, 256), bf16)
    pairs[0:EDGE] = blank
    pairs[EDGE + PAIRS :] = blank

    def place(i, _):
        for z in range(4):
            start = 384 * (z // 2) + 128 * (z % 2)
            value = cost_ref[i, :, start : start + 256]
            if z % 2:
                value = jnp.concatenate([value[:, 64:], value[:, :64]], axis=1)
            pairs[EDGE + z * GROUP + i] = value
        return 0

    lax.fori_loop(0, GROUP, place, 0, unroll=2)

    step = 4
    flat = step * count

    def first(i, _):
        h = i * step
        left = jnp.concatenate(
            [pairs[pl.ds(h + j, step)].reshape(flat, 256) for j in range(3)], axis=1
        )
        for n in range(3):
            lanes = slice(256 * n, 256 * (n + 1))
            value = gelu(mm(left, one_ref[:, lanes]) + bias_one[:, lanes])
            hidden_one[pl.ds(i * (step // 2), step // 2), :, :, lanes] = value.astype(bf16).reshape(
                step // 2, 2, count, 256
            )
        return 0

    lax.fori_loop(0, 76 // step, first, 0)

    def second(i, _):
        h = i * step

        def left(lanes):
            return jnp.concatenate(
                [
                    hidden_one[pl.ds(h + k // 2, step), k % 2, :, lanes].reshape(flat, -1)
                    for k in range(6)
                ],
                axis=1,
            )

        def save(value, lanes):
            hidden_two[pl.ds(i * (step // 2), step // 2), :, :, lanes] = value.astype(bf16).reshape(
                step // 2, 2, count, -1
            )

        for n in range(2):
            value = mm(left(slice(256 * n, 256 * n + 384)), two_ref[...])
            save(gelu(value + bias_two[...]), slice(256 * n, 256 * (n + 1)))
        short = jnp.concatenate([two_ref[384 * k : 384 * k + 256, :128] for k in range(6)], axis=0)
        value = mm(left(slice(512, 768)), short)
        save(gelu(value + bias_two[:, :128]), slice(512, 640))
        return 0

    lax.fori_loop(0, 36 // step, second, 0)

    def third(i, _):
        h = i * step
        for n in range(2):
            left = jnp.concatenate(
                [
                    hidden_two[
                        pl.ds(h + k // 2, step), k % 2, :, 256 * n : 256 * n + 384
                    ].reshape(flat, 384)
                    for k in range(6)
                ],
                axis=1,
            )
            value = mm(left, three_ref[...]) + bias_three[...]
            features[pl.ds(h, step), :, 256 * n : 256 * (n + 1)] = value.astype(bf16).reshape(
                step, count, 256
            )
        return 0

    lax.fori_loop(0, 16 // step, third, 0)

    scale = 1.0 / math.sqrt(128)

    def score(h, peak):
        value = (mm(features[h], query_ref[...]) + pos_ref[pl.ds(h, 1), :]) * scale
        score_ref[h] = value
        return jnp.maximum(peak, value)

    peak = lax.fori_loop(0, 16, score, jnp.full((count, 128), -jnp.inf, f32), unroll=2)
    for k in (8, 16, 32):
        peak = jnp.maximum(peak, pltpu.roll(peak, k, 1))
    low = lax.broadcasted_iota(jnp.int32, (count, 128), 1) < 64

    def weigh(h, total):
        value = jnp.exp(score_ref[h] - peak)
        head = value.astype(bf16).astype(f32)
        score_ref[h] = jnp.where(low, head, value - head)
        return total + value

    total = lax.fori_loop(0, 16, weigh, jnp.zeros((count, 128), f32), unroll=2)
    for k in (8, 16, 32):
        total = total + pltpu.roll(total, k, 1)

    def gather(latent):
        spread = spread_ref[:, 512 * latent : 512 * (latent + 1)]

        def one(h, acc):
            value = mm(score_ref[h].astype(bf16), spread)
            return acc + value * features[h].astype(f32)

        acc = lax.fori_loop(0, 16, one, jnp.zeros((count, 512), f32), unroll=2)
        acc = (acc[:, :128] + acc[:, 128:256]) + (acc[:, 256:384] + acc[:, 384:])
        return acc + pltpu.roll(acc, 64, 1)

    for k in range(4):
        out_ref[:, 128 * k : 128 * (k + 1)] = jnp.where(low, gather(2 * k), gather(2 * k + 1))
    out_ref[:, 512:] = jnp.where(low, peak, total)


def encode(cost, banded, biases, query, pos, spread):
    count = cost.shape[1]
    return pl.pallas_call(
        encode_body,
        out_shape=jax.ShapeDtypeStruct((count, 640), f32),
        scratch_shapes=[
            pltpu.VMEM((PAIRS + 2 * EDGE, count, 256), bf16),
            pltpu.VMEM((38, 2, count, 768), bf16),
            pltpu.VMEM((18, 2, count, 640), bf16),
            pltpu.VMEM((16, count, 512), bf16),
            pltpu.VMEM((16, count, 128), f32),
        ],
        compiler_params=params(),
        name="encode",
    )(cost, *banded, *biases, query, pos, spread)


def combine_body(parts_ref, value_ref, spread_ref, out_ref):
    tiles, count, _ = parts_ref.shape
    low = lax.broadcasted_iota(jnp.int32, (count, 128), 1) < 64
    stats = [parts_ref[t, :, 512:] for t in range(tiles)]
    peak = functools.reduce(jnp.maximum, stats)
    total = jnp.zeros((count, 128), f32)
    weighted = jnp.zeros((count, 512), f32)
    for t in range(tiles):
        factor = jnp.where(low, jnp.exp(stats[t] - peak), 0.0)
        total = total + factor * pltpu.roll(stats[t], 64, 1)
        wide = jnp.dot(factor, spread_ref[...], precision=exact, preferred_element_type=f32)
        weighted = weighted + wide * parts_ref[t, :, :512]
    total = jnp.where(low, total, 1.0)
    share = jnp.where(low, 1.0 / total, 0.0)
    attended = weighted * jnp.dot(share, spread_ref[...], precision=exact, preferred_element_type=f32)
    for latent in range(8):
        part = attended[:, 128 * (latent // 2) : 128 * (latent // 2 + 1)]
        part = jnp.where(low == (latent % 2 == 0), part, 0.0)
        out_ref[:, latent, :] = jnp.dot(
            part, value_ref[...], precision=exact, preferred_element_type=f32
        )


def combine(parts, value_weight):
    lane = jnp.arange(128)[:, None]
    spread = (lane == jnp.arange(512)[None, :] // 64).astype(f32)
    return pl.pallas_call(
        combine_body,
        out_shape=jax.ShapeDtypeStruct((parts.shape[1], 8, 128), f32),
        compiler_params=params(),
        name="combine",
    )(parts, jnp.concatenate([value_weight, value_weight], axis=0), spread)


def spread_to(array, axis):
    peers = lax.axis_size(axis)
    return lax.all_to_all(jnp.broadcast_to(array[None], (peers,) + array.shape), axis, 0, 0)


def on_device(
    target,
    sources,
    kernel_one,
    first_conv_bias,
    kernel_two,
    shift_two,
    kernel_three,
    shift_three,
    latents,
    pos_key,
    w_key,
    value_weight,
):
    tiles = lax.axis_size("tile")
    every = spread_to(sources, "xy")
    rows = lax.all_gather(target, "zh", axis=0)
    width = rows.shape[2]
    up = [(i, i + 1) for i in range(tiles - 1)]
    down = [(j, i) for i, j in up]
    left = lax.ppermute(rows[:, :, width - HALO :], "tile", up)
    right = lax.ppermute(rows[:, :, :HALO], "tile", down)
    cost = cost_maps(rows, left, right, every)
    cost, kernel_one, kernel_two, kernel_three, latents, pos_key = lax.optimization_barrier(
        (cost, kernel_one, kernel_two, kernel_three, latents, pos_key)
    )
    cost = lax.all_to_all(cost, "xy", 0, 0)

    banded = bands(kernel_one, kernel_two, kernel_three)
    query = jnp.dot(latents, w_key.T, precision=exact, preferred_element_type=f32).astype(bf16)
    own = jnp.arange(8)[:, None] == jnp.arange(16)[None, :] % 8
    query = jnp.where(own[:, None, :, None], query.T[None, :, None, :], 0).reshape(512, 128)
    pos = jnp.einsum("ld,hwd->hwl", latents, pos_key, precision=exact).reshape(16, 64)
    pos = jnp.concatenate([pos, pos], axis=1)
    lane = jnp.arange(128)[:, None] % 64
    column = jnp.arange(8 * 512)[None, :]
    spread = (lane == (column % 512) // 64 * 8 + column // 512).astype(bf16)
    biases = (
        jnp.tile(first_conv_bias, 48)[None],
        jnp.tile(shift_two, 8)[None],
        jnp.tile(shift_three, 4)[None],
    )
    parts = encode(cost, banded, biases, query, pos, spread)
    parts = lax.all_to_all(parts.reshape(tiles, -1, parts.shape[1]), "tile", 0, 0)
    tokens = spread_to(combine(parts, value_weight), "tile")
    return tokens.reshape((-1,) + tokens.shape[2:])


def solution(mesh):
    src, tile = mesh.devices.shape
    split = Mesh(mesh.devices.reshape(src // GROUP, GROUP, tile), ("zh", "xy", "tile"))
    rows = ("zh", "xy")
    return jax.shard_map(
        on_device,
        mesh=split,
        in_specs=(
            P(rows, "tile", None),
            P(rows, None),
            P(),
            P(),
            P(),
            P(),
            P(),
            P(),
            P(),
            P(None, "tile", None),
            P(),
            P(),
        ),
        out_specs=P(rows, None, None),
        check_vma=False,
    )
```

```python
import functools
import math

import jax
import jax.numpy as jnp
import numpy as np
from jax import lax
from jax.experimental import pallas as pl
from jax.experimental.pallas import tpu as pltpu
from jax.sharding import Mesh, PartitionSpec as P

exact = lax.Precision.HIGHEST
f32 = jnp.float32
bf16 = jnp.bfloat16

GROUP = 16
HALO = 16
WIDE = 96
PAIRS = 64
EDGE = 7
VMEM = 56 * 1024 * 1024


def params():
    return pltpu.CompilerParams(vmem_limit_bytes=VMEM)


def gelu(x):
    inner = x * (math.sqrt(2.0 / math.pi) + (math.sqrt(2.0 / math.pi) * 0.044715) * (x * x))
    half = 0.5 * x
    return half + half * jnp.tanh(inner)


def nt_dot(a, b):
    return lax.dot_general(a, b, (((1,), (1,)), ((), ())), preferred_element_type=f32)


def mm(a, b):
    return jnp.dot(a, b, preferred_element_type=f32)


def cost_body(rows_ref, left_ref, right_ref, sources_ref, out_ref, *, first):
    parts = []
    for z in range(rows_ref.shape[0]):
        for r in range(2):
            parts += [left_ref[z, r], rows_ref[z, r], right_ref[z, r]]
    window = jnp.concatenate(parts, axis=0)
    groups, count, width = out_ref.shape
    depth = sources_ref.shape[-1]
    mine = sources_ref[:, first : first + count].reshape(groups * count, depth)
    for n in range(0, width, 256):
        value = nt_dot(mine, window[n : n + 256]) * (1.0 / math.sqrt(depth))
        out_ref[:, :, n : n + 256] = value.astype(bf16).reshape(groups, count, 256)


def cost_maps(rows, left, right, sources, first, count):
    return pl.pallas_call(
        functools.partial(cost_body, first=first),
        out_shape=jax.ShapeDtypeStruct((sources.shape[0], count, 2 * WIDE * rows.shape[0]), bf16),
        compiler_params=params(),
        name="cost_maps",
    )(rows, left, right, sources)


def band(kernel_ref, out_ref, step, block):
    _, depth, lanes = kernel_ref.shape
    rows = out_ref.shape[0] // 6
    for t in range(lanes // 128):
        lane = lax.broadcasted_iota(jnp.int32, (depth, 128), 1) // block
        for kh in range(6):
            tile = kernel_ref[kh, :, 128 * t : 128 * (t + 1)].astype(f32)
            total = jnp.zeros((rows, 128), f32)
            for b in range(128 // block):
                top = step * (b + t * (128 // block))
                piece = [jnp.where(lane == b, tile, 0.0)]
                if top:
                    piece = [jnp.zeros((top, 128), f32)] + piece
                if rows - top - depth:
                    piece = piece + [jnp.zeros((rows - top - depth, 128), f32)]
                total = total + jnp.concatenate(piece, axis=0)
            out_ref[kh * rows : (kh + 1) * rows, 128 * t : 128 * (t + 1)] = total.astype(bf16)


def band_body(one_ref, two_ref, three_ref, out_one, out_two, out_three):
    lanes = one_ref.shape[-1]
    row = lax.broadcasted_iota(jnp.int32, (WIDE, lanes), 0)
    tap = row - 2 - 2 * (lax.broadcasted_iota(jnp.int32, (WIDE, lanes), 1) // 16)
    for j in range(3):
        for q in range(2):
            total = jnp.zeros((WIDE, lanes), f32)
            for kw in range(6):
                line = one_ref[2 * j + q, kw : kw + 1, :].astype(f32)
                total = jnp.where(tap == kw, line, total)
            out_one[256 * j + WIDE * q : 256 * j + WIDE * (q + 1), :] = total.astype(bf16)
        out_one[256 * j + 2 * WIDE : 256 * (j + 1), :] = jnp.zeros((256 - 2 * WIDE, lanes), bf16)
    band(two_ref, out_two, 32, 32)
    band(three_ref, out_three, 64, 64)


def bands(kernel_one, kernel_two, kernel_three):
    one = jnp.tile(kernel_one.reshape(6, 6, 16), (1, 1, 48))
    two = jnp.tile(kernel_two.reshape(6, 96, 32), (1, 1, 8))
    three = jnp.tile(kernel_three.reshape(6, 192, 64), (1, 1, 4))
    return pl.pallas_call(
        band_body,
        out_shape=(
            jax.ShapeDtypeStruct((768, 768), bf16),
            jax.ShapeDtypeStruct((2304, 256), bf16),
            jax.ShapeDtypeStruct((2304, 256), bf16),
        ),
        compiler_params=params(),
        name="bands",
    )(one, two, three)


def encode_body(
    cost_ref,
    one_ref,
    two_ref,
    three_ref,
    bias_one,
    bias_two,
    bias_three,
    query_ref,
    pos_ref,
    spread_ref,
    before_ref,
    out_ref,
    pairs,
    hidden_one,
    hidden_two,
    features,
    score_ref,
):
    count = cost_ref.shape[1]
    done = before_ref.shape[0] if before_ref is not None else 0
    blank = jnp.zeros((EDGE, count, 256), bf16)
    pairs[0:EDGE] = blank
    pairs[EDGE + PAIRS :] = blank

    def place(i, _):
        for z in range(4):
            start = 384 * (z // 2) + 128 * (z % 2)
            value = cost_ref[i, :, start : start + 256]
            if z % 2:
                value = jnp.concatenate([value[:, 64:], value[:, :64]], axis=1)
            pairs[EDGE + z * GROUP + i] = value
        return 0

    lax.fori_loop(0, GROUP, place, 0, unroll=2)

    step = 4
    flat = step * count

    def first(i, _):
        h = i * step
        left = jnp.concatenate(
            [pairs[pl.ds(h + j, step)].reshape(flat, 256) for j in range(3)], axis=1
        )
        for n in range(3):
            lanes = slice(256 * n, 256 * (n + 1))
            value = gelu(mm(left, one_ref[:, lanes]) + bias_one[:, lanes])
            hidden_one[pl.ds(i * (step // 2), step // 2), :, :, lanes] = value.astype(bf16).reshape(
                step // 2, 2, count, 256
            )
        return 0

    lax.fori_loop(0, 76 // step, first, 0)

    def second(i, _):
        h = i * step

        def left(lanes):
            return jnp.concatenate(
                [
                    hidden_one[pl.ds(h + k // 2, step), k % 2, :, lanes].reshape(flat, -1)
                    for k in range(6)
                ],
                axis=1,
            )

        def save(value, lanes):
            hidden_two[pl.ds(i * (step // 2), step // 2), :, :, lanes] = value.astype(bf16).reshape(
                step // 2, 2, count, -1
            )

        for n in range(2):
            value = mm(left(slice(256 * n, 256 * n + 384)), two_ref[...])
            save(gelu(value + bias_two[...]), slice(256 * n, 256 * (n + 1)))
        short = jnp.concatenate([two_ref[384 * k : 384 * k + 256, :128] for k in range(6)], axis=0)
        value = mm(left(slice(512, 768)), short)
        save(gelu(value + bias_two[:, :128]), slice(512, 640))
        return 0

    lax.fori_loop(0, 36 // step, second, 0)

    def third(i, _):
        h = i * step
        for n in range(2):
            left = jnp.concatenate(
                [
                    hidden_two[
                        pl.ds(h + k // 2, step), k % 2, :, 256 * n : 256 * n + 384
                    ].reshape(flat, 384)
                    for k in range(6)
                ],
                axis=1,
            )
            value = mm(left, three_ref[...]) + bias_three[...]
            features[pl.ds(h, step), :, 256 * n : 256 * (n + 1)] = value.astype(bf16).reshape(
                step, count, 256
            )
        return 0

    lax.fori_loop(0, 16 // step, third, 0)

    scale = 1.0 / math.sqrt(128)

    def score(h, peak):
        value = (mm(features[h], query_ref[...]) + pos_ref[pl.ds(h, 1), :]) * scale
        score_ref[h] = value
        return jnp.maximum(peak, value)

    peak = lax.fori_loop(0, 16, score, jnp.full((count, 128), -jnp.inf, f32), unroll=2)
    for k in (8, 16, 32):
        peak = jnp.maximum(peak, pltpu.roll(peak, k, 1))
    low = lax.broadcasted_iota(jnp.int32, (count, 128), 1) < 64

    def weigh(h, total):
        value = jnp.exp(score_ref[h] - peak)
        head = value.astype(bf16).astype(f32)
        score_ref[h] = jnp.where(low, head, value - head)
        return total + value

    total = lax.fori_loop(0, 16, weigh, jnp.zeros((count, 128), f32), unroll=2)
    for k in (8, 16, 32):
        total = total + pltpu.roll(total, k, 1)

    def gather(latent):
        spread = spread_ref[:, 512 * latent : 512 * (latent + 1)]

        def one(h, acc):
            value = mm(score_ref[h].astype(bf16), spread)
            return acc + value * features[h].astype(f32)

        acc = lax.fori_loop(0, 16, one, jnp.zeros((count, 512), f32), unroll=2)
        acc = (acc[:, :128] + acc[:, 128:256]) + (acc[:, 256:384] + acc[:, 384:])
        return acc + pltpu.roll(acc, 64, 1)

    for k in range(4):
        out_ref[done:, 128 * k : 128 * (k + 1)] = jnp.where(low, gather(2 * k), gather(2 * k + 1))
    out_ref[done:, 512:] = jnp.where(low, peak, total)
    if done:
        out_ref[:done] = before_ref[...]


def encode(cost, banded, biases, query, pos, spread, before=None):
    count = cost.shape[1]
    whole = count + (0 if before is None else before.shape[0])
    operands = (cost, *banded, *biases, query, pos, spread)

    def body(*refs):
        encode_body(*refs[:10], None, *refs[10:])

    if before is not None:
        body, operands = (encode_body, operands + (before,))
    return pl.pallas_call(
        body,
        out_shape=jax.ShapeDtypeStruct((whole, 640), f32),
        scratch_shapes=[
            pltpu.VMEM((PAIRS + 2 * EDGE, count, 256), bf16),
            pltpu.VMEM((38, 2, count, 768), bf16),
            pltpu.VMEM((18, 2, count, 640), bf16),
            pltpu.VMEM((16, count, 512), bf16),
            pltpu.VMEM((16, count, 128), f32),
        ],
        compiler_params=params(),
        name="encode",
    )(*operands)


def combine_body(parts_ref, spread_ref, out_ref):
    tiles, count, _ = parts_ref.shape
    low = lax.broadcasted_iota(jnp.int32, (count, 128), 1) < 64
    stats = [parts_ref[t, :, 512:] for t in range(tiles)]
    peak = functools.reduce(jnp.maximum, stats)
    factors = [jnp.where(low, jnp.exp(stat - peak), 0.0) for stat in stats]
    totals = [factor * pltpu.roll(stat, 64, 1) for factor, stat in zip(factors, stats)]
    total = jnp.where(low, functools.reduce(jnp.add, totals), 1.0)
    shares = jnp.concatenate([factor / total for factor in factors], axis=0)
    wide = jnp.dot(shares, spread_ref[...], precision=exact, preferred_element_type=f32)
    attended = jnp.zeros((count, 512), f32)
    for t in range(tiles):
        attended = attended + wide[count * t : count * (t + 1)] * parts_ref[t, :, :512]
    for t in range(tiles):
        out_ref[t] = attended


def combine(parts, spread):
    return pl.pallas_call(
        combine_body,
        out_shape=jax.ShapeDtypeStruct(parts.shape[:2] + (512,), f32),
        compiler_params=params(),
        name="combine",
    )(parts, spread)


def value_body(attended_ref, value_ref, out_ref):
    low = lax.broadcasted_iota(jnp.int32, (attended_ref.shape[0], 128), 1) < 64
    for latent in range(8):
        part = attended_ref[:, 128 * (latent // 2) : 128 * (latent // 2 + 1)]
        part = jnp.where(low == (latent % 2 == 0), part, 0.0)
        out_ref[:, latent, :] = jnp.dot(
            part, value_ref[...], precision=exact, preferred_element_type=f32
        )


def valued(attended, value_weight):
    return pl.pallas_call(
        value_body,
        out_shape=jax.ShapeDtypeStruct((attended.shape[0], 8, 128), f32),
        compiler_params=params(),
        name="valued",
    )(attended, value_weight)


def prepare(
    kernel_one, kernel_two, kernel_three, latents, pos_key, first_conv_bias, shift_two, shift_three, w_key
):
    banded = bands(kernel_one, kernel_two, kernel_three)
    query = jnp.dot(latents, w_key.T, precision=exact, preferred_element_type=f32).astype(bf16)
    own = np.arange(8)[:, None] == np.arange(16)[None, :] % 8
    query = query.T[None, :, None, :] * own[:, None, :, None].astype(bf16)
    query = query.reshape(512, 128)
    pos = jnp.einsum("ld,hwd->hwl", latents, pos_key, precision=exact).reshape(16, 64)
    pos = jnp.concatenate([pos, pos], axis=1)
    lane = np.arange(128)[:, None] % 64
    column = np.arange(8 * 512)[None, :]
    spread = jnp.asarray((lane == (column % 512) // 64 * 8 + column // 512).astype(bf16))
    biases = (
        jnp.tile(first_conv_bias, 48)[None],
        jnp.tile(shift_two, 8)[None],
        jnp.tile(shift_three, 4)[None],
    )
    return banded, biases, query, pos, spread


def on_device(
    target,
    sources,
    kernel_one,
    first_conv_bias,
    kernel_two,
    shift_two,
    kernel_three,
    shift_three,
    latents,
    pos_key,
    w_key,
    value_weight,
):
    tiles = lax.axis_size("tile")
    groups = lax.axis_size("xy")
    copies = jnp.broadcast_to(sources[None], (groups,) + sources.shape)
    copies, target = lax.optimization_barrier((copies, target))
    every = lax.all_to_all(copies, "xy", 0, 0)
    rows = lax.all_gather(target, "zh", axis=0)
    width = rows.shape[2]
    up = [(i, i + 1) for i in range(tiles - 1)]
    down = [(j, i) for i, j in up]
    left = lax.ppermute(rows[:, :, width - HALO :], "tile", up)
    right = lax.ppermute(rows[:, :, :HALO], "tile", down)
    half = sources.shape[0] // 2
    cost = cost_maps(rows, left, right, every, 0, half)
    weights = (kernel_one, kernel_two, kernel_three, latents, pos_key)
    cost, weights = lax.optimization_barrier((cost, weights))
    prepared = prepare(*weights, first_conv_bias, shift_two, shift_three, w_key)
    other = cost_maps(rows, left, right, every, half, half)
    cost = lax.all_to_all(cost, "xy", 0, 0)
    other, prepared = lax.optimization_barrier((other, prepared))
    other = lax.all_to_all(other, "xy", 0, 0)
    parts = encode(cost, *prepared)
    parts = encode(other, *prepared, parts)
    parts = lax.all_to_all(parts.reshape(tiles, -1, parts.shape[1]), "tile", 0, 0)
    latent = np.arange(128)[:, None]
    spread = jnp.asarray((latent == np.arange(512)[None, :] // 64).astype(np.float32))
    attended = lax.all_to_all(combine(parts, spread), "tile", 0, 0)
    value_weight = jnp.concatenate([value_weight, value_weight], axis=0)
    return valued(attended.reshape(-1, attended.shape[-1]), value_weight)


def solution(mesh):
    src, tile = mesh.devices.shape
    split = Mesh(mesh.devices.reshape(src // GROUP, GROUP, tile), ("zh", "xy", "tile"))
    rows = ("zh", "xy")
    return jax.shard_map(
        on_device,
        mesh=split,
        in_specs=(
            P(rows, "tile", None),
            P(rows, None),
            P(),
            P(),
            P(),
            P(),
            P(),
            P(),
            P(),
            P(None, "tile", None),
            P(),
            P(),
        ),
        out_specs=P(rows, None, None),
        check_vma=False,
    )
```

```python
import functools
import math

import jax
import jax.numpy as jnp
import numpy as np
from jax import lax
from jax.experimental import pallas as pl
from jax.experimental.pallas import tpu as pltpu
from jax.sharding import Mesh, PartitionSpec as P

exact = lax.Precision.HIGHEST
f32 = jnp.float32
bf16 = jnp.bfloat16

GROUP = 16
HALO = 16
WIDE = 96
PAIRS = 64
EDGE = 7
VMEM = 56 * 1024 * 1024
ROWS_ONE = 38
ROWS_TWO = 18
ROWS_THREE = 16


def params():
    return pltpu.CompilerParams(vmem_limit_bytes=VMEM)


def gelu(x):
    inner = x * (math.sqrt(2.0 / math.pi) + (math.sqrt(2.0 / math.pi) * 0.044715) * (x * x))
    half = 0.5 * x
    return half + half * jnp.tanh(inner)


def nt_dot(a, b):
    return lax.dot_general(a, b, (((1,), (1,)), ((), ())), preferred_element_type=f32)


def mm(a, b):
    return jnp.dot(a, b, preferred_element_type=f32)


def cost_body(rows_ref, left_ref, right_ref, sources_ref, out_ref, *, first):
    parts = []
    for z in range(rows_ref.shape[0]):
        for r in range(2):
            parts += [left_ref[z, r], rows_ref[z, r], right_ref[z, r]]
    window = jnp.concatenate(parts, axis=0)
    groups, count, width = out_ref.shape
    depth = sources_ref.shape[-1]
    mine = sources_ref[:, first : first + count].reshape(groups * count, depth)
    for n in range(0, width, 256):
        value = nt_dot(mine, window[n : n + 256]) * (1.0 / math.sqrt(depth))
        out_ref[:, :, n : n + 256] = value.astype(bf16).reshape(groups, count, 256)


def cost_maps(rows, left, right, sources, first, count):
    return pl.pallas_call(
        functools.partial(cost_body, first=first),
        out_shape=jax.ShapeDtypeStruct((sources.shape[0], count, 2 * WIDE * rows.shape[0]), bf16),
        compiler_params=params(),
        name="cost_maps",
    )(rows, left, right, sources)


def band(kernel_ref, out_ref, step, block):
    _, depth, lanes = kernel_ref.shape
    rows = out_ref.shape[0] // 6
    for t in range(lanes // 128):
        lane = lax.broadcasted_iota(jnp.int32, (depth, 128), 1) // block
        for kh in range(6):
            tile = kernel_ref[kh, :, 128 * t : 128 * (t + 1)].astype(f32)
            total = jnp.zeros((rows, 128), f32)
            for b in range(128 // block):
                top = step * (b + t * (128 // block))
                piece = [jnp.where(lane == b, tile, 0.0)]
                if top:
                    piece = [jnp.zeros((top, 128), f32)] + piece
                if rows - top - depth:
                    piece = piece + [jnp.zeros((rows - top - depth, 128), f32)]
                total = total + jnp.concatenate(piece, axis=0)
            out_ref[kh * rows : (kh + 1) * rows, 128 * t : 128 * (t + 1)] = total.astype(bf16)


def band_body(one_ref, two_ref, three_ref, out_one, out_two, out_three):
    lanes = one_ref.shape[-1]
    row = lax.broadcasted_iota(jnp.int32, (WIDE, lanes), 0)
    tap = row - 2 - 2 * (lax.broadcasted_iota(jnp.int32, (WIDE, lanes), 1) // 16)
    for j in range(3):
        for q in range(2):
            total = jnp.zeros((WIDE, lanes), f32)
            for kw in range(6):
                line = one_ref[2 * j + q, kw : kw + 1, :].astype(f32)
                total = jnp.where(tap == kw, line, total)
            out_one[256 * j + WIDE * q : 256 * j + WIDE * (q + 1), :] = total.astype(bf16)
        out_one[256 * j + 2 * WIDE : 256 * (j + 1), :] = jnp.zeros((256 - 2 * WIDE, lanes), bf16)
    band(two_ref, out_two, 32, 32)
    band(three_ref, out_three, 64, 64)


def bands(kernel_one, kernel_two, kernel_three):
    one = jnp.tile(kernel_one.reshape(6, 6, 16), (1, 1, 48))
    two = jnp.tile(kernel_two.reshape(6, 96, 32), (1, 1, 8))
    three = jnp.tile(kernel_three.reshape(6, 192, 64), (1, 1, 4))
    return pl.pallas_call(
        band_body,
        out_shape=(
            jax.ShapeDtypeStruct((768, 768), bf16),
            jax.ShapeDtypeStruct((2304, 256), bf16),
            jax.ShapeDtypeStruct((2304, 256), bf16),
        ),
        compiler_params=params(),
        name="bands",
    )(one, two, three)


def encode_body(
    cost_ref,
    one_ref,
    two_ref,
    three_ref,
    bias_one,
    bias_two,
    bias_three,
    query_ref,
    pos_ref,
    spread_ref,
    before_ref,
    out_ref,
    pairs,
    hidden_one,
    hidden_two,
    features,
    score_ref,
):
    count = cost_ref.shape[1]
    done = before_ref.shape[0] if before_ref is not None else 0
    blank = jnp.zeros((EDGE, count, 256), bf16)
    pairs[0:EDGE] = blank
    pairs[EDGE + PAIRS : 2 * EDGE + PAIRS] = blank

    def place(i, _):
        for z in range(4):
            start = 384 * (z // 2) + 128 * (z % 2)
            value = cost_ref[i, :, start : start + 256]
            if z % 2:
                value = jnp.concatenate([value[:, 64:], value[:, :64]], axis=1)
            pairs[EDGE + z * GROUP + i] = value
        return 0

    lax.fori_loop(0, GROUP, place, 0, unroll=2)

    def first(i, _):
        step = ROWS_ONE
        h = i * step
        left = jnp.concatenate(
            [pairs[pl.ds(h + j, step)].reshape(step * count, 256) for j in range(3)], axis=1
        )
        for n in range(3):
            lanes = slice(256 * n, 256 * (n + 1))
            value = gelu(mm(left, one_ref[:, lanes]) + bias_one[:, lanes])
            hidden_one[pl.ds(i * (step // 2), step // 2), :, :, lanes] = value.astype(bf16).reshape(
                step // 2, 2, count, 256
            )
        return 0

    lax.fori_loop(0, pl.cdiv(76, ROWS_ONE), first, 0)

    def taps(source, h, step, lanes):
        parts = [
            source[pl.ds(h + k // 2, step), k % 2, :, lanes].reshape(step * count, -1)
            for k in range(6)
        ]
        return jnp.concatenate(parts, axis=1)

    short = jnp.concatenate([two_ref[384 * k : 384 * k + 256, :128] for k in range(6)], axis=0)

    def second(i, _):
        step = ROWS_TWO
        h = i * step
        for n in range(3):
            lanes = slice(256 * n, min(256 * n + 384, 768))
            right, bias = (two_ref[...], bias_two[...])
            if n == 2:
                right, bias = (short, bias_two[:, :128])
            value = gelu(mm(taps(hidden_one, h, step, lanes), right) + bias)
            lanes = slice(256 * n, 256 * n + value.shape[1])
            hidden_two[pl.ds(i * (step // 2), step // 2), :, :, lanes] = value.astype(bf16).reshape(
                step // 2, 2, count, -1
            )
        return 0

    lax.fori_loop(0, 36 // ROWS_TWO, second, 0)

    def third(i, _):
        step = ROWS_THREE
        h = i * step
        for n in range(2):
            left = taps(hidden_two, h, step, slice(256 * n, 256 * n + 384))
            value = mm(left, three_ref[...]) + bias_three[...]
            features[pl.ds(h, step), :, 256 * n : 256 * (n + 1)] = value.astype(bf16).reshape(
                step, count, 256
            )
        return 0

    lax.fori_loop(0, 16 // ROWS_THREE, third, 0)

    scale = 1.0 / math.sqrt(128)

    value = mm(features[...].reshape(16 * count, 512), query_ref[...]).reshape(16, count, 128)
    value = (value + pos_ref[...][:, None, :]) * scale
    score_ref[...] = value
    peak = jnp.max(value, axis=0)
    for k in (8, 16, 32):
        peak = jnp.maximum(peak, pltpu.roll(peak, k, 1))
    low = lax.broadcasted_iota(jnp.int32, (count, 128), 1) < 64

    value = jnp.exp(score_ref[...] - peak)
    total = jnp.sum(value, axis=0)
    head = value.astype(bf16).astype(f32)
    shares = jnp.where(low, head, value - head).astype(bf16).reshape(16 * count, 128)
    for k in (8, 16, 32):
        total = total + pltpu.roll(total, k, 1)

    def gather(latent):
        spread = spread_ref[:, 512 * latent : 512 * (latent + 1)]

        value = mm(shares, spread).reshape(16, count, 512)
        acc = jnp.sum(value * features[...].astype(f32), axis=0)
        acc = (acc[:, :128] + acc[:, 128:256]) + (acc[:, 256:384] + acc[:, 384:])
        return acc + pltpu.roll(acc, 64, 1)

    for k in range(4):
        out_ref[done:, 128 * k : 128 * (k + 1)] = jnp.where(low, gather(2 * k), gather(2 * k + 1))
    out_ref[done:, 512:] = jnp.where(low, peak, total)
    if done:
        out_ref[:done] = before_ref[...]


def encode(cost, banded, biases, query, pos, spread, before=None):
    count = cost.shape[1]
    whole = count + (0 if before is None else before.shape[0])
    operands = (cost, *banded, *biases, query, pos, spread)

    def body(*refs):
        encode_body(*refs[:10], None, *refs[10:])

    if before is not None:
        body, operands = (encode_body, operands + (before,))
    return pl.pallas_call(
        body,
        out_shape=jax.ShapeDtypeStruct((whole, 640), f32),
        scratch_shapes=[
            pltpu.VMEM((pl.cdiv(76, ROWS_ONE) * ROWS_ONE + 2, count, 256), bf16),
            pltpu.VMEM((pl.cdiv(76, ROWS_ONE) * (ROWS_ONE // 2), 2, count, 768), bf16),
            pltpu.VMEM((18, 2, count, 640), bf16),
            pltpu.VMEM((16, count, 512), bf16),
            pltpu.VMEM((16, count, 128), f32),
        ],
        compiler_params=params(),
        name="encode",
    )(*operands)


def combine_body(parts_ref, spread_ref, out_ref):
    tiles, count, _ = parts_ref.shape
    low = lax.broadcasted_iota(jnp.int32, (count, 128), 1) < 64
    stats = [parts_ref[t, :, 512:] for t in range(tiles)]
    peak = functools.reduce(jnp.maximum, stats)
    factors = [jnp.where(low, jnp.exp(stat - peak), 0.0) for stat in stats]
    totals = [factor * pltpu.roll(stat, 64, 1) for factor, stat in zip(factors, stats)]
    total = jnp.where(low, functools.reduce(jnp.add, totals), 1.0)
    shares = jnp.concatenate([factor / total for factor in factors], axis=0)
    wide = jnp.dot(shares, spread_ref[...], precision=exact, preferred_element_type=f32)
    attended = jnp.zeros((count, 512), f32)
    for t in range(tiles):
        attended = attended + wide[count * t : count * (t + 1)] * parts_ref[t, :, :512]
    for t in range(tiles):
        out_ref[t] = attended


def combine(parts, spread):
    return pl.pallas_call(
        combine_body,
        out_shape=jax.ShapeDtypeStruct(parts.shape[:2] + (512,), f32),
        compiler_params=params(),
        name="combine",
    )(parts, spread)


def value_body(attended_ref, value_ref, out_ref):
    low = lax.broadcasted_iota(jnp.int32, (attended_ref.shape[0], 128), 1) < 64
    for latent in range(8):
        part = attended_ref[:, 128 * (latent // 2) : 128 * (latent // 2 + 1)]
        part = jnp.where(low == (latent % 2 == 0), part, 0.0)
        out_ref[:, latent, :] = jnp.dot(
            part, value_ref[...], precision=exact, preferred_element_type=f32
        )


def valued(attended, value_weight):
    return pl.pallas_call(
        value_body,
        out_shape=jax.ShapeDtypeStruct((attended.shape[0], 8, 128), f32),
        compiler_params=params(),
        name="valued",
    )(attended, value_weight)


def prepare(
    kernel_one, kernel_two, kernel_three, latents, pos_key, first_conv_bias, shift_two, shift_three, w_key
):
    banded = bands(kernel_one, kernel_two, kernel_three)
    query = jnp.dot(latents, w_key.T, precision=exact, preferred_element_type=f32).astype(bf16)
    own = np.arange(8)[:, None] == np.arange(16)[None, :] % 8
    query = query.T[None, :, None, :] * own[:, None, :, None].astype(bf16)
    query = query.reshape(512, 128)
    pos = jnp.einsum("ld,hwd->hwl", latents, pos_key, precision=exact).reshape(16, 64)
    pos = jnp.concatenate([pos, pos], axis=1)
    lane = np.arange(128)[:, None] % 64
    column = np.arange(8 * 512)[None, :]
    spread = jnp.asarray((lane == (column % 512) // 64 * 8 + column // 512).astype(bf16))
    biases = (
        jnp.tile(first_conv_bias, 48)[None],
        jnp.tile(shift_two, 8)[None],
        jnp.tile(shift_three, 4)[None],
    )
    return banded, biases, query, pos, spread


def on_device(
    target,
    sources,
    kernel_one,
    first_conv_bias,
    kernel_two,
    shift_two,
    kernel_three,
    shift_three,
    latents,
    pos_key,
    w_key,
    value_weight,
):
    tiles = lax.axis_size("tile")
    groups = lax.axis_size("xy")
    copies = jnp.broadcast_to(sources[None], (groups,) + sources.shape)
    copies, target = lax.optimization_barrier((copies, target))
    every = lax.all_to_all(copies, "xy", 0, 0)
    rows = lax.all_gather(target, "zh", axis=0)
    width = rows.shape[2]
    up = [(i, i + 1) for i in range(tiles - 1)]
    down = [(j, i) for i, j in up]
    left = lax.ppermute(rows[:, :, width - HALO :], "tile", up)
    right = lax.ppermute(rows[:, :, :HALO], "tile", down)
    cost = cost_maps(rows, left, right, every, 0, sources.shape[0])
    weights = (kernel_one, kernel_two, kernel_three, latents, pos_key)
    cost, weights = lax.optimization_barrier((cost, weights))
    prepared = prepare(*weights, first_conv_bias, shift_two, shift_three, w_key)
    parts = encode(lax.all_to_all(cost, "xy", 0, 0), *prepared)
    parts = lax.all_to_all(parts.reshape(tiles, -1, parts.shape[1]), "tile", 0, 0)
    latent = np.arange(128)[:, None]
    spread = jnp.asarray((latent == np.arange(512)[None, :] // 64).astype(np.float32))
    attended = lax.all_to_all(combine(parts, spread), "tile", 0, 0)
    value_weight = jnp.concatenate([value_weight, value_weight], axis=0)
    return valued(attended.reshape(-1, attended.shape[-1]), value_weight)


def solution(mesh):
    src, tile = mesh.devices.shape
    split = Mesh(mesh.devices.reshape(src // GROUP, GROUP, tile), ("zh", "xy", "tile"))
    rows = ("zh", "xy")
    return jax.shard_map(
        on_device,
        mesh=split,
        in_specs=(
            P(rows, "tile", None),
            P(rows, None),
            P(),
            P(),
            P(),
            P(),
            P(),
            P(),
            P(),
            P(None, "tile", None),
            P(),
            P(),
        ),
        out_specs=P(rows, None, None),
        check_vma=False,
    )
```

```python
import functools
import math

import jax
import jax.numpy as jnp
import numpy as np
from jax import lax
from jax.experimental import pallas as pl
from jax.experimental.pallas import tpu as pltpu
from jax.sharding import Mesh, PartitionSpec as P

exact = lax.Precision.HIGHEST
f32 = jnp.float32
bf16 = jnp.bfloat16

GROUP = 16
HALO = 16
WIDE = 96
PAIRS = 64
EDGE = 7
ROWS_ONE = 38
ROWS_TWO = 18
ROWS_THREE = 16


def call(body, out_shape, operands, name, limit, scratch=()):
    near = pl.BlockSpec(memory_space=pltpu.VMEM)
    return pl.pallas_call(
        body,
        out_shape=out_shape,
        in_specs=[near] * len(operands),
        out_specs=jax.tree.map(lambda _: near, out_shape),
        scratch_shapes=scratch,
        compiler_params=pltpu.CompilerParams(vmem_limit_bytes=limit * 1024 * 1024),
        name=name,
    )(*(pltpu.with_memory_space_constraint(x, pltpu.VMEM) for x in operands))


def vmem(shape, dtype):
    return pltpu.VMEM(shape, dtype)


def gelu(x):
    inner = x * (math.sqrt(2.0 / math.pi) + (math.sqrt(2.0 / math.pi) * 0.044715) * (x * x))
    half = 0.5 * x
    return half + half * jnp.tanh(inner)


def nt_dot(a, b):
    return lax.dot_general(a, b, (((1,), (1,)), ((), ())), preferred_element_type=f32)


def mm(a, b):
    return jnp.dot(a, b, preferred_element_type=f32)


def cost_body(rows_ref, left_ref, right_ref, sources_ref, out_ref, *, first):
    parts = []
    for z in range(rows_ref.shape[0]):
        for r in range(2):
            parts += [left_ref[z, r], rows_ref[z, r], right_ref[z, r]]
    window = jnp.concatenate(parts, axis=0)
    groups, count, width = out_ref.shape
    depth = sources_ref.shape[-1]
    mine = sources_ref[:, first : first + count].reshape(groups * count, depth)
    for n in range(0, width, 256):
        value = nt_dot(mine, window[n : n + 256]) * (1.0 / math.sqrt(depth))
        out_ref[:, :, n : n + 256] = value.astype(bf16).reshape(groups, count, 256)


def cost_maps(rows, left, right, sources, first, count):
    return call(
        functools.partial(cost_body, first=first),
        vmem((sources.shape[0], count, 2 * WIDE * rows.shape[0]), bf16),
        (rows, left, right, sources),
        "cost_maps",
        16,
    )


def band(kernel_ref, out_ref, step, block):
    _, depth, lanes = kernel_ref.shape
    rows = out_ref.shape[0] // 6
    for t in range(lanes // 128):
        lane = lax.broadcasted_iota(jnp.int32, (depth, 128), 1) // block
        for kh in range(6):
            tile = kernel_ref[kh, :, 128 * t : 128 * (t + 1)].astype(f32)
            total = jnp.zeros((rows, 128), f32)
            for b in range(128 // block):
                top = step * (b + t * (128 // block))
                piece = [jnp.where(lane == b, tile, 0.0)]
                if top:
                    piece = [jnp.zeros((top, 128), f32)] + piece
                if rows - top - depth:
                    piece = piece + [jnp.zeros((rows - top - depth, 128), f32)]
                total = total + jnp.concatenate(piece, axis=0)
            out_ref[kh * rows : (kh + 1) * rows, 128 * t : 128 * (t + 1)] = total.astype(bf16)


def band_body(one_ref, two_ref, three_ref, out_one, out_two, out_three):
    lanes = one_ref.shape[-1]
    row = lax.broadcasted_iota(jnp.int32, (WIDE, lanes), 0)
    tap = row - 2 - 2 * (lax.broadcasted_iota(jnp.int32, (WIDE, lanes), 1) // 16)
    for j in range(3):
        for q in range(2):
            total = jnp.zeros((WIDE, lanes), f32)
            for kw in range(6):
                line = one_ref[2 * j + q, kw : kw + 1, :].astype(f32)
                total = jnp.where(tap == kw, line, total)
            out_one[256 * j + WIDE * q : 256 * j + WIDE * (q + 1), :] = total.astype(bf16)
        out_one[256 * j + 2 * WIDE : 256 * (j + 1), :] = jnp.zeros((256 - 2 * WIDE, lanes), bf16)
    band(two_ref, out_two, 32, 32)
    band(three_ref, out_three, 64, 64)


def bands(kernel_one, kernel_two, kernel_three):
    one = jnp.tile(kernel_one.reshape(6, 6, 16), (1, 1, 48))
    two = jnp.tile(kernel_two.reshape(6, 96, 32), (1, 1, 8))
    three = jnp.tile(kernel_three.reshape(6, 192, 64), (1, 1, 4))
    shapes = (vmem((768, 768), bf16), vmem((2304, 256), bf16), vmem((2304, 256), bf16))
    return call(band_body, shapes, (one, two, three), "bands", 16)


def encode_body(
    cost_ref,
    one_ref,
    two_ref,
    three_ref,
    bias_one,
    bias_two,
    bias_three,
    query_ref,
    pos_ref,
    spread_ref,
    before_ref,
    out_ref,
    pairs,
    hidden_one,
    hidden_two,
    features,
    score_ref,
):
    count = cost_ref.shape[1]
    done = before_ref.shape[0] if before_ref is not None else 0
    blank = jnp.zeros((EDGE, count, 256), bf16)
    pairs[0:EDGE] = blank
    pairs[EDGE + PAIRS : 2 * EDGE + PAIRS] = blank

    def place(i, _):
        for z in range(4):
            start = 384 * (z // 2) + 128 * (z % 2)
            value = cost_ref[i, :, start : start + 256]
            if z % 2:
                value = jnp.concatenate([value[:, 64:], value[:, :64]], axis=1)
            pairs[EDGE + z * GROUP + i] = value
        return 0

    lax.fori_loop(0, GROUP, place, 0, unroll=2)

    def first(i, _):
        step = ROWS_ONE
        h = i * step
        left = jnp.concatenate(
            [pairs[pl.ds(h + j, step)].reshape(step * count, 256) for j in range(3)], axis=1
        )
        for n in range(3):
            lanes = slice(256 * n, 256 * (n + 1))
            value = gelu(mm(left, one_ref[:, lanes]) + bias_one[:, lanes])
            hidden_one[pl.ds(i * (step // 2), step // 2), :, :, lanes] = value.astype(bf16).reshape(
                step // 2, 2, count, 256
            )
        return 0

    lax.fori_loop(0, pl.cdiv(76, ROWS_ONE), first, 0)

    def taps(source, h, step, lanes):
        parts = [
            source[pl.ds(h + k // 2, step), k % 2, :, lanes].reshape(step * count, -1)
            for k in range(6)
        ]
        return jnp.concatenate(parts, axis=1)

    short = jnp.concatenate([two_ref[384 * k : 384 * k + 256, :128] for k in range(6)], axis=0)

    def second(i, _):
        step = ROWS_TWO
        h = i * step
        for n in range(3):
            lanes = slice(256 * n, min(256 * n + 384, 768))
            right, bias = (two_ref[...], bias_two[...])
            if n == 2:
                right, bias = (short, bias_two[:, :128])
            value = gelu(mm(taps(hidden_one, h, step, lanes), right) + bias)
            lanes = slice(256 * n, 256 * n + value.shape[1])
            hidden_two[pl.ds(i * (step // 2), step // 2), :, :, lanes] = value.astype(bf16).reshape(
                step // 2, 2, count, -1
            )
        return 0

    lax.fori_loop(0, 36 // ROWS_TWO, second, 0)

    def third(i, _):
        step = ROWS_THREE
        h = i * step
        for n in range(2):
            left = taps(hidden_two, h, step, slice(256 * n, 256 * n + 384))
            value = mm(left, three_ref[...]) + bias_three[...]
            features[pl.ds(h, step), :, 256 * n : 256 * (n + 1)] = value.astype(bf16).reshape(
                step, count, 256
            )
        return 0

    lax.fori_loop(0, 16 // ROWS_THREE, third, 0)

    scale = 1.0 / math.sqrt(128)

    value = mm(features[...].reshape(16 * count, 512), query_ref[...]).reshape(16, count, 128)
    value = (value + pos_ref[...][:, None, :]) * scale
    score_ref[...] = value
    peak = jnp.max(value, axis=0)
    for k in (8, 16, 32):
        peak = jnp.maximum(peak, pltpu.roll(peak, k, 1))
    low = lax.broadcasted_iota(jnp.int32, (count, 128), 1) < 64

    value = jnp.exp(score_ref[...] - peak)
    total = jnp.sum(value, axis=0)
    head = value.astype(bf16).astype(f32)
    shares = jnp.where(low, head, value - head).astype(bf16).reshape(16 * count, 128)
    for k in (8, 16, 32):
        total = total + pltpu.roll(total, k, 1)

    def gather(latent):
        spread = spread_ref[:, 512 * latent : 512 * (latent + 1)]

        value = mm(shares, spread).reshape(16, count, 512)
        acc = jnp.sum(value * features[...].astype(f32), axis=0)
        acc = (acc[:, :128] + acc[:, 128:256]) + (acc[:, 256:384] + acc[:, 384:])
        return acc + pltpu.roll(acc, 64, 1)

    for k in range(4):
        out_ref[done:, 128 * k : 128 * (k + 1)] = jnp.where(low, gather(2 * k), gather(2 * k + 1))
    out_ref[done:, 512:] = jnp.where(low, peak, total)
    if done:
        out_ref[:done] = before_ref[...]


def encode(cost, banded, biases, query, pos, spread, before=None):
    count = cost.shape[1]
    whole = count + (0 if before is None else before.shape[0])
    operands = (cost, *banded, *biases, query, pos, spread)

    def body(*refs):
        encode_body(*refs[:10], None, *refs[10:])

    if before is not None:
        body, operands = (encode_body, operands + (before,))
    scratch = [
        vmem((pl.cdiv(76, ROWS_ONE) * ROWS_ONE + 2, count, 256), bf16),
        vmem((pl.cdiv(76, ROWS_ONE) * (ROWS_ONE // 2), 2, count, 768), bf16),
        vmem((18, 2, count, 640), bf16),
        vmem((16, count, 512), bf16),
        vmem((16, count, 128), f32),
    ]
    return call(body, vmem((whole, 640), f32), operands, "encode", 40, scratch)


def combine_body(parts_ref, spread_ref, out_ref):
    tiles, count, _ = parts_ref.shape
    low = lax.broadcasted_iota(jnp.int32, (count, 128), 1) < 64
    stats = [parts_ref[t, :, 512:] for t in range(tiles)]
    peak = functools.reduce(jnp.maximum, stats)
    factors = [jnp.where(low, jnp.exp(stat - peak), 0.0) for stat in stats]
    totals = [factor * pltpu.roll(stat, 64, 1) for factor, stat in zip(factors, stats)]
    total = jnp.where(low, functools.reduce(jnp.add, totals), 1.0)
    shares = jnp.concatenate([factor / total for factor in factors], axis=0)
    wide = jnp.dot(shares, spread_ref[...], precision=exact, preferred_element_type=f32)
    attended = jnp.zeros((count, 512), f32)
    for t in range(tiles):
        attended = attended + wide[count * t : count * (t + 1)] * parts_ref[t, :, :512]
    for t in range(tiles):
        out_ref[t] = attended


def combine(parts, spread):
    return call(
        combine_body, vmem(parts.shape[:2] + (512,), f32), (parts, spread), "combine", 8
    )


def value_body(attended_ref, value_ref, out_ref):
    low = lax.broadcasted_iota(jnp.int32, (attended_ref.shape[0], 128), 1) < 64
    for latent in range(8):
        part = attended_ref[:, 128 * (latent // 2) : 128 * (latent // 2 + 1)]
        part = jnp.where(low == (latent % 2 == 0), part, 0.0)
        out_ref[:, latent, :] = jnp.dot(
            part, value_ref[...], precision=exact, preferred_element_type=f32
        )


def valued(attended, value_weight):
    shape = jax.ShapeDtypeStruct((attended.shape[0], 8, 128), f32)
    return call(value_body, shape, (attended, value_weight), "valued", 8)


def prepare(
    kernel_one, kernel_two, kernel_three, latents, pos_key, first_conv_bias, shift_two, shift_three, w_key
):
    banded = bands(kernel_one, kernel_two, kernel_three)
    query = jnp.dot(latents, w_key.T, precision=exact, preferred_element_type=f32).astype(bf16)
    own = np.arange(8)[:, None] == np.arange(16)[None, :] % 8
    query = query.T[None, :, None, :] * own[:, None, :, None].astype(bf16)
    query = query.reshape(512, 128)
    pos = jnp.einsum("ld,hwd->hwl", latents, pos_key, precision=exact).reshape(16, 64)
    pos = jnp.concatenate([pos, pos], axis=1)
    lane = np.arange(128)[:, None] % 64
    column = np.arange(8 * 512)[None, :]
    spread = jnp.asarray((lane == (column % 512) // 64 * 8 + column // 512).astype(bf16))
    biases = (
        jnp.tile(first_conv_bias, 48)[None],
        jnp.tile(shift_two, 8)[None],
        jnp.tile(shift_three, 4)[None],
    )
    return banded, biases, query, pos, spread


def on_device(
    target,
    sources,
    kernel_one,
    first_conv_bias,
    kernel_two,
    shift_two,
    kernel_three,
    shift_three,
    latents,
    pos_key,
    w_key,
    value_weight,
):
    tiles = lax.axis_size("tile")
    groups = lax.axis_size("xy")
    copies = jnp.broadcast_to(sources[None], (groups,) + sources.shape)
    copies, target = lax.optimization_barrier((copies, target))
    every = lax.all_to_all(copies, "xy", 0, 0)
    rows = lax.all_gather(target, "zh", axis=0)
    width = rows.shape[2]
    up = [(i, i + 1) for i in range(tiles - 1)]
    down = [(j, i) for i, j in up]
    left = lax.ppermute(rows[:, :, width - HALO :], "tile", up)
    right = lax.ppermute(rows[:, :, :HALO], "tile", down)
    cost = cost_maps(rows, left, right, every, 0, sources.shape[0])
    weights = (kernel_one, kernel_two, kernel_three, latents, pos_key)
    cost, weights = lax.optimization_barrier((cost, weights))
    prepared = prepare(*weights, first_conv_bias, shift_two, shift_three, w_key)
    parts = encode(lax.all_to_all(cost, "xy", 0, 0), *prepared)
    parts = lax.all_to_all(parts.reshape(tiles, -1, parts.shape[1]), "tile", 0, 0)
    latent = np.arange(128)[:, None]
    spread = jnp.asarray((latent == np.arange(512)[None, :] // 64).astype(np.float32))
    attended = lax.all_to_all(combine(parts, spread), "tile", 0, 0)
    value_weight = jnp.concatenate([value_weight, value_weight], axis=0)
    return valued(attended.reshape(-1, attended.shape[-1]), value_weight)


def solution(mesh):
    src, tile = mesh.devices.shape
    split = Mesh(mesh.devices.reshape(src // GROUP, GROUP, tile), ("zh", "xy", "tile"))
    rows = ("zh", "xy")
    return jax.shard_map(
        on_device,
        mesh=split,
        in_specs=(
            P(rows, "tile", None),
            P(rows, None),
            P(),
            P(),
            P(),
            P(),
            P(),
            P(),
            P(),
            P(None, "tile", None),
            P(),
            P(),
        ),
        out_specs=P(rows, None, None),
        check_vma=False,
    )
```

```python
import functools
import math

import jax
import jax.numpy as jnp
import numpy as np
from jax import lax
from jax.experimental import pallas as pl
from jax.experimental.pallas import tpu as pltpu
from jax.sharding import Mesh, PartitionSpec as P

exact = lax.Precision.HIGHEST
f32 = jnp.float32
bf16 = jnp.bfloat16

GROUP = 16
HALO = 16
OWN = 512
PAIRS = 64
EDGE = 7
ROWS_ONE = 38
ROWS_TWO = 18
ROWS_THREE = 16


def call(body, out_shape, operands, name, limit, scratch=()):
    near = pl.BlockSpec(memory_space=pltpu.VMEM)
    return pl.pallas_call(
        body,
        out_shape=out_shape,
        in_specs=[near] * len(operands),
        out_specs=jax.tree.map(lambda _: near, out_shape),
        scratch_shapes=scratch,
        compiler_params=pltpu.CompilerParams(vmem_limit_bytes=limit * 1024 * 1024),
        name=name,
    )(*(pltpu.with_memory_space_constraint(x, pltpu.VMEM) for x in operands))


def vmem(shape, dtype):
    return pltpu.VMEM(shape, dtype)


def gelu(x):
    inner = x * (math.sqrt(2.0 / math.pi) + (math.sqrt(2.0 / math.pi) * 0.044715) * (x * x))
    half = 0.5 * x
    return half + half * jnp.tanh(inner)


def nt_dot(a, b):
    return lax.dot_general(a, b, (((1,), (1,)), ((), ())), preferred_element_type=f32)


def mm(a, b):
    return jnp.dot(a, b, preferred_element_type=f32)


def cost_of(sources_ref, window, out_ref, start):
    groups, count, depth = sources_ref.shape
    every = sources_ref[...].reshape(groups * count, depth)
    for n in range(0, window.shape[0], 256):
        value = nt_dot(every, window[n : n + 256]) * (1.0 / math.sqrt(depth))
        out_ref[:, :, start + n : start + n + 256] = value.astype(bf16).reshape(groups, count, 256)


def own_body(rows_ref, sources_ref, out_ref):
    parts = []
    for z in range(rows_ref.shape[0]):
        for half in (slice(0, 32), slice(32, 64)):
            parts += [rows_ref[z, 0, half], rows_ref[z, 1, half]]
    cost_of(sources_ref, jnp.concatenate(parts, axis=0), out_ref, 0)


def halo_body(left_ref, right_ref, sources_ref, own_ref, out_ref):
    out_ref[:, :, :OWN] = own_ref[...]
    parts = []
    for z in range(left_ref.shape[0]):
        for r in range(2):
            parts += [left_ref[z, r], right_ref[z, r]]
    cost_of(sources_ref, jnp.concatenate(parts, axis=0), out_ref, OWN)


def cost_maps(rows, left, right, sources):
    own = call(own_body, vmem(sources.shape[:2] + (OWN,), bf16), (rows, sources), "own_columns", 16)
    shape = vmem(sources.shape[:2] + (OWN + OWN // 2,), bf16)
    return call(halo_body, shape, (left, right, sources, own), "halo_columns", 16)


def band(kernel_ref, out_ref, step, block):
    _, depth, lanes = kernel_ref.shape
    rows = out_ref.shape[0] // 6
    for t in range(lanes // 128):
        lane = lax.broadcasted_iota(jnp.int32, (depth, 128), 1) // block
        for kh in range(6):
            tile = kernel_ref[kh, :, 128 * t : 128 * (t + 1)].astype(f32)
            total = jnp.zeros((rows, 128), f32)
            for b in range(128 // block):
                top = step * (b + t * (128 // block))
                piece = [jnp.where(lane == b, tile, 0.0)]
                if top:
                    piece = [jnp.zeros((top, 128), f32)] + piece
                if rows - top - depth:
                    piece = piece + [jnp.zeros((rows - top - depth, 128), f32)]
                total = total + jnp.concatenate(piece, axis=0)
            out_ref[kh * rows : (kh + 1) * rows, 128 * t : 128 * (t + 1)] = total.astype(bf16)


def band_body(one_ref, two_ref, three_ref, out_one, out_two, out_three):
    row = lax.broadcasted_iota(jnp.int32, (128, 256), 0)
    place = lax.broadcasted_iota(jnp.int32, (128, 256), 1) // 16
    odd = (row // 32) % 2 == 1
    x = row % 32
    upper = row >= 64
    halo = jnp.where(x < 16, x - 16, x + 48)
    columns = (
        jnp.where(upper, halo, x),
        jnp.where(upper, x + 32, x),
        jnp.where(upper, x + 32, halo),
    )
    for n in range(3):
        tap = columns[n] + 14 - 2 * (place + 16 * n)
        for j in range(3):
            total = jnp.zeros((128, 256), f32)
            for kw in range(6):
                first = one_ref[2 * j, kw : kw + 1, :].astype(f32)
                second = one_ref[2 * j + 1, kw : kw + 1, :].astype(f32)
                total = jnp.where(tap == kw, jnp.where(odd, second, first), total)
            out_one[128 * j : 128 * (j + 1), 256 * n : 256 * (n + 1)] = total.astype(bf16)
    band(two_ref, out_two, 32, 32)
    band(three_ref, out_three, 64, 64)


def bands(kernel_one, kernel_two, kernel_three):
    one = jnp.tile(kernel_one.reshape(6, 6, 16), (1, 1, 16))
    two = jnp.tile(kernel_two.reshape(6, 96, 32), (1, 1, 8))
    three = jnp.tile(kernel_three.reshape(6, 192, 64), (1, 1, 4))
    shapes = (vmem((384, 768), bf16), vmem((2304, 256), bf16), vmem((2304, 256), bf16))
    return call(band_body, shapes, (one, two, three), "bands", 16)


def encode_body(
    cost_ref,
    one_ref,
    two_ref,
    three_ref,
    bias_one,
    bias_two,
    bias_three,
    query_ref,
    pos_ref,
    spread_ref,
    before_ref,
    out_ref,
    pairs,
    hidden_one,
    hidden_two,
    features,
    score_ref,
):
    count = cost_ref.shape[1]
    done = before_ref.shape[0] if before_ref is not None else 0
    blank = jnp.zeros((EDGE, count, 384), bf16)
    pairs[0:EDGE] = blank
    pairs[EDGE + PAIRS : 2 * EDGE + PAIRS] = blank

    def place(i, _):
        for z in range(4):
            own = cost_ref[i, :, 128 * z : 128 * (z + 1)]
            halo = cost_ref[i, :, OWN + 64 * z : OWN + 64 * (z + 1)]
            pairs[EDGE + z * GROUP + i] = jnp.concatenate(
                [own[:, :64], halo, own, halo, own[:, 64:]], axis=1
            )
        return 0

    lax.fori_loop(0, GROUP, place, 0, unroll=2)

    def first(i, _):
        step = ROWS_ONE
        h = i * step
        for n in range(3):
            lanes = slice(128 * n, 128 * (n + 1))
            left = jnp.concatenate(
                [pairs[pl.ds(h + j, step), :, lanes].reshape(step * count, 128) for j in range(3)],
                axis=1,
            )
            lanes = slice(256 * n, 256 * (n + 1))
            value = gelu(mm(left, one_ref[:, lanes]) + bias_one[:, lanes])
            hidden_one[pl.ds(i * (step // 2), step // 2), :, :, lanes] = value.astype(bf16).reshape(
                step // 2, 2, count, 256
            )
        return 0

    lax.fori_loop(0, pl.cdiv(76, ROWS_ONE), first, 0)

    def taps(source, h, step, lanes):
        parts = [
            source[pl.ds(h + k // 2, step), k % 2, :, lanes].reshape(step * count, -1)
            for k in range(6)
        ]
        return jnp.concatenate(parts, axis=1)

    short = jnp.concatenate([two_ref[384 * k : 384 * k + 256, :128] for k in range(6)], axis=0)

    def second(i, _):
        step = ROWS_TWO
        h = i * step
        for n in range(3):
            lanes = slice(256 * n, min(256 * n + 384, 768))
            right, bias = (two_ref[...], bias_two[...])
            if n == 2:
                right, bias = (short, bias_two[:, :128])
            value = gelu(mm(taps(hidden_one, h, step, lanes), right) + bias)
            lanes = slice(256 * n, 256 * n + value.shape[1])
            hidden_two[pl.ds(i * (step // 2), step // 2), :, :, lanes] = value.astype(bf16).reshape(
                step // 2, 2, count, -1
            )
        return 0

    lax.fori_loop(0, 36 // ROWS_TWO, second, 0)

    def third(i, _):
        step = ROWS_THREE
        h = i * step
        for n in range(2):
            left = taps(hidden_two, h, step, slice(256 * n, 256 * n + 384))
            value = mm(left, three_ref[...]) + bias_three[...]
            features[pl.ds(h, step), :, 256 * n : 256 * (n + 1)] = value.astype(bf16).reshape(
                step, count, 256
            )
        return 0

    lax.fori_loop(0, 16 // ROWS_THREE, third, 0)

    scale = 1.0 / math.sqrt(128)

    value = mm(features[...].reshape(16 * count, 512), query_ref[...]).reshape(16, count, 128)
    value = (value + pos_ref[...][:, None, :]) * scale
    score_ref[...] = value
    peak = jnp.max(value, axis=0)
    for k in (8, 16, 32):
        peak = jnp.maximum(peak, pltpu.roll(peak, k, 1))
    low = lax.broadcasted_iota(jnp.int32, (count, 128), 1) < 64

    value = jnp.exp(score_ref[...] - peak)
    total = jnp.sum(value, axis=0)
    head = value.astype(bf16).astype(f32)
    shares = jnp.where(low, head, value - head).astype(bf16).reshape(16 * count, 128)
    for k in (8, 16, 32):
        total = total + pltpu.roll(total, k, 1)

    def gather(latent):
        spread = spread_ref[:, 512 * latent : 512 * (latent + 1)]

        value = mm(shares, spread).reshape(16, count, 512)
        acc = jnp.sum(value * features[...].astype(f32), axis=0)
        acc = (acc[:, :128] + acc[:, 128:256]) + (acc[:, 256:384] + acc[:, 384:])
        return acc + pltpu.roll(acc, 64, 1)

    for k in range(4):
        out_ref[done:, 128 * k : 128 * (k + 1)] = jnp.where(low, gather(2 * k), gather(2 * k + 1))
    out_ref[done:, 512:] = jnp.where(low, peak, total)
    if done:
        out_ref[:done] = before_ref[...]


def encode(cost, banded, biases, query, pos, spread, before=None):
    count = cost.shape[1]
    whole = count + (0 if before is None else before.shape[0])
    operands = (cost, *banded, *biases, query, pos, spread)

    def body(*refs):
        encode_body(*refs[:10], None, *refs[10:])

    if before is not None:
        body, operands = (encode_body, operands + (before,))
    scratch = [
        vmem((pl.cdiv(76, ROWS_ONE) * ROWS_ONE + 2, count, 384), bf16),
        vmem((pl.cdiv(76, ROWS_ONE) * (ROWS_ONE // 2), 2, count, 768), bf16),
        vmem((18, 2, count, 640), bf16),
        vmem((16, count, 512), bf16),
        vmem((16, count, 128), f32),
    ]
    return call(body, vmem((whole, 640), f32), operands, "encode", 40, scratch)


def combine_body(parts_ref, spread_ref, out_ref):
    tiles, count, _ = parts_ref.shape
    low = lax.broadcasted_iota(jnp.int32, (count, 128), 1) < 64
    stats = [parts_ref[t, :, 512:] for t in range(tiles)]
    peak = functools.reduce(jnp.maximum, stats)
    factors = [jnp.where(low, jnp.exp(stat - peak), 0.0) for stat in stats]
    totals = [factor * pltpu.roll(stat, 64, 1) for factor, stat in zip(factors, stats)]
    total = jnp.where(low, functools.reduce(jnp.add, totals), 1.0)
    shares = jnp.concatenate([factor / total for factor in factors], axis=0)
    wide = jnp.dot(shares, spread_ref[...], precision=exact, preferred_element_type=f32)
    attended = jnp.zeros((count, 512), f32)
    for t in range(tiles):
        attended = attended + wide[count * t : count * (t + 1)] * parts_ref[t, :, :512]
    for t in range(tiles):
        out_ref[t] = attended


def combine(parts, spread):
    return call(
        combine_body, vmem(parts.shape[:2] + (512,), f32), (parts, spread), "combine", 8
    )


def value_body(attended_ref, value_ref, out_ref):
    count = attended_ref.shape[0]
    low = lax.broadcasted_iota(jnp.int32, (count, 128), 1) < 64
    parts = []
    for latent in range(8):
        part = attended_ref[:, 128 * (latent // 2) : 128 * (latent // 2 + 1)]
        parts.append(jnp.where(low == (latent % 2 == 0), part, 0.0))
    value = jnp.dot(
        jnp.concatenate(parts, axis=0),
        value_ref[...],
        precision=exact,
        preferred_element_type=f32,
    )
    for latent in range(8):
        out_ref[:, latent, :] = value[count * latent : count * (latent + 1)]


def valued(attended, value_weight):
    shape = jax.ShapeDtypeStruct((attended.shape[0], 8, 128), f32)
    return call(value_body, shape, (attended, value_weight), "valued", 8)


def prepare(
    kernel_one, kernel_two, kernel_three, latents, pos_key, first_conv_bias, shift_two, shift_three, w_key
):
    banded = bands(kernel_one, kernel_two, kernel_three)
    query = jnp.dot(latents, w_key.T, precision=exact, preferred_element_type=f32).astype(bf16)
    own = np.arange(8)[:, None] == np.arange(16)[None, :] % 8
    query = query.T[None, :, None, :] * own[:, None, :, None].astype(bf16)
    query = query.reshape(512, 128)
    pos = jnp.einsum("ld,hwd->hwl", latents, pos_key, precision=exact).reshape(16, 64)
    pos = jnp.concatenate([pos, pos], axis=1)
    lane = np.arange(128)[:, None] % 64
    column = np.arange(8 * 512)[None, :]
    spread = jnp.asarray((lane == (column % 512) // 64 * 8 + column // 512).astype(bf16))
    biases = (
        jnp.tile(first_conv_bias, 48)[None],
        jnp.tile(shift_two, 8)[None],
        jnp.tile(shift_three, 4)[None],
    )
    return banded, biases, query, pos, spread


def on_device(
    target,
    sources,
    kernel_one,
    first_conv_bias,
    kernel_two,
    shift_two,
    kernel_three,
    shift_three,
    latents,
    pos_key,
    w_key,
    value_weight,
):
    tiles = lax.axis_size("tile")
    groups = lax.axis_size("xy")
    copies = jnp.broadcast_to(sources[None], (groups,) + sources.shape)
    copies, target = lax.optimization_barrier((copies, target))
    every = lax.all_to_all(copies, "xy", 0, 0)
    rows = lax.all_gather(target, "zh", axis=0)
    width = rows.shape[2]
    up = [(i, i + 1) for i in range(tiles - 1)]
    down = [(j, i) for i, j in up]
    left = lax.ppermute(rows[:, :, width - HALO :], "tile", up)
    right = lax.ppermute(rows[:, :, :HALO], "tile", down)
    cost = cost_maps(rows, left, right, every)
    weights = (kernel_one, kernel_two, kernel_three, latents, pos_key)
    cost, weights, value_weight = lax.optimization_barrier((cost, weights, value_weight))
    value_weight = jnp.concatenate([value_weight, value_weight], axis=0)
    prepared = prepare(*weights, first_conv_bias, shift_two, shift_three, w_key)
    parts = encode(lax.all_to_all(cost, "xy", 0, 0), *prepared)
    parts, value_weight = lax.optimization_barrier((parts, value_weight))
    parts = lax.all_to_all(parts.reshape(tiles, -1, parts.shape[1]), "tile", 0, 0)
    latent = np.arange(128)[:, None]
    spread = jnp.asarray((latent == np.arange(512)[None, :] // 64).astype(np.float32))
    attended = lax.all_to_all(combine(parts, spread), "tile", 0, 0)
    return valued(attended.reshape(-1, attended.shape[-1]), value_weight)


def solution(mesh):
    src, tile = mesh.devices.shape
    split = Mesh(mesh.devices.reshape(src // GROUP, GROUP, tile), ("zh", "xy", "tile"))
    rows = ("zh", "xy")
    return jax.shard_map(
        on_device,
        mesh=split,
        in_specs=(
            P(rows, "tile", None),
            P(rows, None),
            P(),
            P(),
            P(),
            P(),
            P(),
            P(),
            P(),
            P(None, "tile", None),
            P(),
            P(),
        ),
        out_specs=P(rows, None, None),
        check_vma=False,
    )
```

```python
import functools
import math

import jax
import jax.numpy as jnp
import numpy as np
from jax import lax
from jax.experimental import pallas as pl
from jax.experimental.pallas import tpu as pltpu
from jax.sharding import Mesh, PartitionSpec as P

exact = lax.Precision.HIGHEST
f32 = jnp.float32
bf16 = jnp.bfloat16

GROUP = 16
HALO = 16
OWN = 512
PAIRS = 64
EDGE = 7
ROWS_ONE = 38
ROWS_TWO = 18
ROWS_THREE = 16


def call(body, out_shape, operands, name, limit, scratch=(), far=()):
    near = pl.BlockSpec(memory_space=pltpu.VMEM)
    hbm = pl.BlockSpec(memory_space=pltpu.HBM)
    operands = [
        pltpu.with_memory_space_constraint(x, pltpu.HBM if i in far else pltpu.VMEM)
        for i, x in enumerate(operands)
    ]
    return pl.pallas_call(
        body,
        out_shape=out_shape,
        in_specs=[hbm if i in far else near for i in range(len(operands))],
        out_specs=jax.tree.map(lambda _: near, out_shape),
        scratch_shapes=scratch,
        compiler_params=pltpu.CompilerParams(vmem_limit_bytes=limit * 1024 * 1024),
        name=name,
    )(*operands)


def vmem(shape, dtype):
    return pltpu.VMEM(shape, dtype)


def gelu(x):
    inner = x * (math.sqrt(2.0 / math.pi) + (math.sqrt(2.0 / math.pi) * 0.044715) * (x * x))
    half = 0.5 * x
    return half + half * jnp.tanh(inner)


def nt_dot(a, b):
    return lax.dot_general(a, b, (((1,), (1,)), ((), ())), preferred_element_type=f32)


def mm(a, b):
    return jnp.dot(a, b, preferred_element_type=f32)


def cost_of(sources_ref, window, out_ref, start):
    groups, count, depth = sources_ref.shape
    every = sources_ref[...].reshape(groups * count, depth)
    for n in range(0, window.shape[0], 256):
        value = nt_dot(every, window[n : n + 256]) * (1.0 / math.sqrt(depth))
        out_ref[:, :, start + n : start + n + 256] = value.astype(bf16).reshape(groups, count, 256)


def own_body(rows_ref, sources_ref, out_ref):
    parts = []
    for z in range(rows_ref.shape[0]):
        for half in (slice(0, 32), slice(32, 64)):
            parts += [rows_ref[z, 0, half], rows_ref[z, 1, half]]
    cost_of(sources_ref, jnp.concatenate(parts, axis=0), out_ref, 0)


def halo_body(left_ref, right_ref, sources_ref, own_ref, out_ref):
    out_ref[:, :, :OWN] = own_ref[...]
    parts = []
    for z in range(left_ref.shape[0]):
        for r in range(2):
            parts += [left_ref[z, r], right_ref[z, r]]
    cost_of(sources_ref, jnp.concatenate(parts, axis=0), out_ref, OWN)


def cost_maps(rows, left, right, sources):
    own = call(own_body, vmem(sources.shape[:2] + (OWN,), bf16), (rows, sources), "own_columns", 16)
    shape = vmem(sources.shape[:2] + (OWN + OWN // 2,), bf16)
    return call(halo_body, shape, (left, right, sources, own), "halo_columns", 16)


def band(taps, out_ref, step, block):
    depth = taps.shape[0] // 6
    rows = out_ref.shape[0] // 6
    for t in range(taps.shape[1] // 128):
        lane = lax.broadcasted_iota(jnp.int32, (depth, 128), 1) // block
        for kh in range(6):
            tile = taps[depth * kh : depth * (kh + 1), 128 * t : 128 * (t + 1)]
            total = jnp.zeros((rows, 128), f32)
            for b in range(128 // block):
                top = step * (b + t * (128 // block))
                piece = [jnp.where(lane == b, tile, 0.0)]
                if top:
                    piece = [jnp.zeros((top, 128), f32)] + piece
                if rows - top - depth:
                    piece = piece + [jnp.zeros((rows - top - depth, 128), f32)]
                total = total + jnp.concatenate(piece, axis=0)
            out_ref[kh * rows : (kh + 1) * rows, 128 * t : 128 * (t + 1)] = total.astype(bf16)


def repeated(kernel_ref):
    width = kernel_ref.shape[1]
    row = lax.broadcasted_iota(jnp.int32, (width, 256), 0)
    lane = lax.broadcasted_iota(jnp.int32, (width, 256), 1)
    pick = jnp.where(lane % width == row, 1.0, 0.0).astype(bf16)
    return mm(kernel_ref[...], pick)


def band_body(
    one_ref,
    two_ref,
    three_ref,
    latents_ref,
    key_ref,
    pos_key_ref,
    out_one,
    out_two,
    out_three,
    out_query,
    out_pos,
):
    row = lax.broadcasted_iota(jnp.int32, (128, 256), 0)
    place = lax.broadcasted_iota(jnp.int32, (128, 256), 1) // 16
    odd = (row // 32) % 2 == 1
    x = row % 32
    upper = row >= 64
    halo = jnp.where(x < 16, x - 16, x + 48)
    columns = (
        jnp.where(upper, halo, x),
        jnp.where(upper, x + 32, x),
        jnp.where(upper, x + 32, halo),
    )
    one = repeated(one_ref)
    for n in range(3):
        tap = columns[n] + 14 - 2 * (place + 16 * n)
        for j in range(3):
            total = jnp.zeros((128, 256), f32)
            for kw in range(6):
                first = one[12 * j + kw : 12 * j + kw + 1]
                second = one[12 * j + 6 + kw : 12 * j + 7 + kw]
                total = jnp.where(tap == kw, jnp.where(odd, second, first), total)
            out_one[128 * j : 128 * (j + 1), 256 * n : 256 * (n + 1)] = total.astype(bf16)
    band(repeated(two_ref), out_two, 32, 32)
    band(repeated(three_ref), out_three, 64, 64)

    def exact_nt(a, b):
        return lax.dot_general(
            a, b, (((1,), (1,)), ((), ())), precision=exact, preferred_element_type=f32
        )

    latents = jnp.concatenate([latents_ref[...]] * 16, axis=0)
    query = exact_nt(key_ref[...], latents)
    patch = lax.broadcasted_iota(jnp.int32, (64, 128), 1) // 8 % 8
    for w in range(8):
        out_query[64 * w : 64 * (w + 1), :] = jnp.where(patch == w, query, 0.0).astype(bf16)
    pos = exact_nt(pos_key_ref[...].reshape(128, 128), latents)
    row = lax.broadcasted_iota(jnp.int32, (128, 128), 0)
    patch = lax.broadcasted_iota(jnp.int32, (128, 128), 1) // 8
    pos = jnp.where(patch % 8 == row % 8, pos, 0.0)
    out_pos[...] = jnp.sum(pos.reshape(16, 8, 128), axis=1)


def bands(kernel_one, kernel_two, kernel_three, latents, w_key, pos_key):
    shapes = (
        jax.ShapeDtypeStruct((384, 768), bf16),
        jax.ShapeDtypeStruct((2304, 256), bf16),
        jax.ShapeDtypeStruct((2304, 256), bf16),
        jax.ShapeDtypeStruct((512, 128), bf16),
        jax.ShapeDtypeStruct((16, 128), f32),
    )
    kernels = (
        kernel_one.reshape(36, 16),
        kernel_two.reshape(6 * 96, 32),
        kernel_three.reshape(6 * 192, 64),
    )
    return call(band_body, shapes, kernels + (latents, w_key, pos_key), "bands", 16)


def encode_body(
    cost_ref,
    one_far,
    two_far,
    three_far,
    query_ref,
    pos_ref,
    bias_one,
    bias_two,
    bias_three,
    spread_far,
    out_ref,
    pairs,
    hidden_one,
    hidden_two,
    features,
    score_ref,
    one_ref,
    two_ref,
    three_ref,
    spread_ref,
    arrived,
):
    count = cost_ref.shape[1]
    fetches = [
        pltpu.make_async_copy(far, near, arrived.at[i])
        for i, (far, near) in enumerate(
            (
                (one_far, one_ref),
                (two_far, two_ref),
                (three_far, three_ref),
                (spread_far, spread_ref),
            )
        )
    ]
    for fetch in fetches:
        fetch.start()
    blank = jnp.zeros((EDGE, count, 384), bf16)
    pairs[0:EDGE] = blank
    pairs[EDGE + PAIRS : 2 * EDGE + PAIRS] = blank

    def place(i, _):
        for z in range(4):
            own = cost_ref[i, :, 128 * z : 128 * (z + 1)]
            halo = cost_ref[i, :, OWN + 64 * z : OWN + 64 * (z + 1)]
            pairs[EDGE + z * GROUP + i] = jnp.concatenate(
                [own[:, :64], halo, own, halo, own[:, 64:]], axis=1
            )
        return 0

    lax.fori_loop(0, GROUP, place, 0, unroll=2)

    def first(i, _):
        step = ROWS_ONE
        h = i * step
        for n in range(3):
            lanes = slice(128 * n, 128 * (n + 1))
            left = jnp.concatenate(
                [pairs[pl.ds(h + j, step), :, lanes].reshape(step * count, 128) for j in range(3)],
                axis=1,
            )
            lanes = slice(256 * n, 256 * (n + 1))
            value = gelu(mm(left, one_ref[:, lanes]) + bias_one[:, lanes])
            hidden_one[pl.ds(i * (step // 2), step // 2), :, :, lanes] = value.astype(bf16).reshape(
                step // 2, 2, count, 256
            )
        return 0

    fetches[0].wait()
    lax.fori_loop(0, pl.cdiv(76, ROWS_ONE), first, 0)
    fetches[1].wait()

    def taps(source, h, step, lanes):
        parts = [
            source[pl.ds(h + k // 2, step), k % 2, :, lanes].reshape(step * count, -1)
            for k in range(6)
        ]
        return jnp.concatenate(parts, axis=1)

    short = jnp.concatenate([two_ref[384 * k : 384 * k + 256, :128] for k in range(6)], axis=0)

    def second(i, _):
        step = ROWS_TWO
        h = i * step
        for n in range(3):
            lanes = slice(256 * n, min(256 * n + 384, 768))
            right, bias = (two_ref[...], bias_two[...])
            if n == 2:
                right, bias = (short, bias_two[:, :128])
            value = gelu(mm(taps(hidden_one, h, step, lanes), right) + bias)
            lanes = slice(256 * n, 256 * n + value.shape[1])
            hidden_two[pl.ds(i * (step // 2), step // 2), :, :, lanes] = value.astype(bf16).reshape(
                step // 2, 2, count, -1
            )
        return 0

    lax.fori_loop(0, 36 // ROWS_TWO, second, 0)

    def third(i, _):
        step = ROWS_THREE
        h = i * step
        for n in range(2):
            left = taps(hidden_two, h, step, slice(256 * n, 256 * n + 384))
            value = mm(left, three_ref[...]) + bias_three[...]
            features[pl.ds(h, step), :, 256 * n : 256 * (n + 1)] = value.astype(bf16).reshape(
                step, count, 256
            )
        return 0

    fetches[2].wait()
    lax.fori_loop(0, 16 // ROWS_THREE, third, 0)
    fetches[3].wait()

    scale = 1.0 / math.sqrt(128)

    value = mm(features[...].reshape(16 * count, 512), query_ref[...]).reshape(16, count, 128)
    value = (value + pos_ref[...][:, None, :]) * scale
    score_ref[...] = value
    peak = jnp.max(value, axis=0)
    for k in (8, 16, 32):
        peak = jnp.maximum(peak, pltpu.roll(peak, k, 1))
    low = lax.broadcasted_iota(jnp.int32, (count, 128), 1) < 64

    value = jnp.exp(score_ref[...] - peak)
    total = jnp.sum(value, axis=0)
    head = value.astype(bf16).astype(f32)
    shares = jnp.where(low, head, value - head).astype(bf16).reshape(16 * count, 128)
    for k in (8, 16, 32):
        total = total + pltpu.roll(total, k, 1)

    def gather(latent):
        spread = spread_ref[:, 512 * latent : 512 * (latent + 1)]

        value = mm(shares, spread).reshape(16, count, 512)
        acc = jnp.sum(value * features[...].astype(f32), axis=0)
        acc = (acc[:, :128] + acc[:, 128:256]) + (acc[:, 256:384] + acc[:, 384:])
        return acc + pltpu.roll(acc, 64, 1)

    for k in range(4):
        out_ref[:, 128 * k : 128 * (k + 1)] = jnp.where(low, gather(2 * k), gather(2 * k + 1))
    out_ref[:, 512:] = jnp.where(low, peak, total)


def encode(cost, prepared, biases, spread):
    count = cost.shape[1]
    scratch = [
        vmem((pl.cdiv(76, ROWS_ONE) * ROWS_ONE + 2, count, 384), bf16),
        vmem((pl.cdiv(76, ROWS_ONE) * (ROWS_ONE // 2), 2, count, 768), bf16),
        vmem((18, 2, count, 640), bf16),
        vmem((16, count, 512), bf16),
        vmem((16, count, 128), f32),
        vmem((384, 768), bf16),
        vmem((2304, 256), bf16),
        vmem((2304, 256), bf16),
        vmem((128, 4096), bf16),
        pltpu.SemaphoreType.DMA((4,)),
    ]
    operands = (cost, *prepared, *biases, spread)
    shape = vmem((count, 640), f32)
    return call(encode_body, shape, operands, "encode", 40, scratch, far=(1, 2, 3, 9))


def combine_body(parts_ref, spread_ref, out_ref):
    tiles, count, _ = parts_ref.shape
    low = lax.broadcasted_iota(jnp.int32, (count, 128), 1) < 64
    stats = [parts_ref[t, :, 512:] for t in range(tiles)]
    peak = functools.reduce(jnp.maximum, stats)
    factors = [jnp.where(low, jnp.exp(stat - peak), 0.0) for stat in stats]
    totals = [factor * pltpu.roll(stat, 64, 1) for factor, stat in zip(factors, stats)]
    total = jnp.where(low, functools.reduce(jnp.add, totals), 1.0)
    shares = jnp.concatenate([factor / total for factor in factors], axis=0)
    wide = jnp.dot(shares, spread_ref[...], precision=exact, preferred_element_type=f32)
    attended = jnp.zeros((count, 512), f32)
    for t in range(tiles):
        attended = attended + wide[count * t : count * (t + 1)] * parts_ref[t, :, :512]
    for t in range(tiles):
        out_ref[t] = attended


def combine(parts, spread):
    return call(
        combine_body, vmem(parts.shape[:2] + (512,), f32), (parts, spread), "combine", 8
    )


def value_body(attended_ref, value_ref, out_ref):
    count = attended_ref.shape[0]
    low = lax.broadcasted_iota(jnp.int32, (count, 128), 1) < 64
    parts = []
    for latent in range(8):
        part = attended_ref[:, 128 * (latent // 2) : 128 * (latent // 2 + 1)]
        parts.append(jnp.where(low == (latent % 2 == 0), part, 0.0))
    value = jnp.dot(
        jnp.concatenate(parts, axis=0),
        value_ref[...],
        precision=exact,
        preferred_element_type=f32,
    )
    for latent in range(8):
        out_ref[:, latent, :] = value[count * latent : count * (latent + 1)]


def valued(attended, value_weight):
    shape = jax.ShapeDtypeStruct((attended.shape[0], 8, 128), f32)
    return call(value_body, shape, (attended, value_weight), "valued", 8)


def prepare(
    kernel_one, kernel_two, kernel_three, latents, pos_key, first_conv_bias, shift_two, shift_three, w_key
):
    prepared = bands(kernel_one, kernel_two, kernel_three, latents, w_key, pos_key)
    lane = np.arange(128)[:, None] % 64
    column = np.arange(8 * 512)[None, :]
    spread = jnp.asarray((lane == (column % 512) // 64 * 8 + column // 512).astype(bf16))
    biases = (
        jnp.tile(first_conv_bias, 48)[None],
        jnp.tile(shift_two, 8)[None],
        jnp.tile(shift_three, 4)[None],
    )
    return prepared, biases, spread


def on_device(
    target,
    sources,
    kernel_one,
    first_conv_bias,
    kernel_two,
    shift_two,
    kernel_three,
    shift_three,
    latents,
    pos_key,
    w_key,
    value_weight,
):
    tiles = lax.axis_size("tile")
    groups = lax.axis_size("xy")
    copies = jnp.broadcast_to(sources[None], (groups,) + sources.shape)
    copies, target = lax.optimization_barrier((copies, target))
    every = lax.all_to_all(copies, "xy", 0, 0)
    rows = lax.all_gather(target, "zh", axis=0)
    width = rows.shape[2]
    up = [(i, i + 1) for i in range(tiles - 1)]
    down = [(j, i) for i, j in up]
    left = lax.ppermute(rows[:, :, width - HALO :], "tile", up)
    right = lax.ppermute(rows[:, :, :HALO], "tile", down)
    cost = cost_maps(rows, left, right, every)
    weights = (kernel_one, kernel_two, kernel_three, latents, pos_key)
    cost, weights, value_weight = lax.optimization_barrier((cost, weights, value_weight))
    value_weight = jnp.concatenate([value_weight, value_weight], axis=0)
    prepared = prepare(*weights, first_conv_bias, shift_two, shift_three, w_key)
    parts = encode(lax.all_to_all(cost, "xy", 0, 0), *prepared)
    parts, value_weight = lax.optimization_barrier((parts, value_weight))
    parts = lax.all_to_all(parts.reshape(tiles, -1, parts.shape[1]), "tile", 0, 0)
    latent = np.arange(128)[:, None]
    spread = jnp.asarray((latent == np.arange(512)[None, :] // 64).astype(np.float32))
    attended = lax.all_to_all(combine(parts, spread), "tile", 0, 0)
    return valued(attended.reshape(-1, attended.shape[-1]), value_weight)


def solution(mesh):
    src, tile = mesh.devices.shape
    split = Mesh(mesh.devices.reshape(src // GROUP, GROUP, tile), ("zh", "xy", "tile"))
    rows = ("zh", "xy")
    return jax.shard_map(
        on_device,
        mesh=split,
        in_specs=(
            P(rows, "tile", None),
            P(rows, None),
            P(),
            P(),
            P(),
            P(),
            P(),
            P(),
            P(),
            P(None, "tile", None),
            P(),
            P(),
        ),
        out_specs=P(rows, None, None),
        check_vma=False,
    )
```

```python
import functools
import math

import jax
import jax.numpy as jnp
import numpy as np
from jax import lax
from jax.experimental import pallas as pl
from jax.experimental.pallas import tpu as pltpu
from jax.sharding import Mesh, PartitionSpec as P

exact = lax.Precision.HIGHEST
f32 = jnp.float32
bf16 = jnp.bfloat16

GROUP = 16
HALO = 16
OWN = 512
PAIRS = 64
EDGE = 7
ROWS_ONE = 38
ROWS_TWO = 18
ROWS_THREE = 16


def call(body, out_shape, operands, name, limit, scratch=(), far=()):
    near = pl.BlockSpec(memory_space=pltpu.VMEM)
    hbm = pl.BlockSpec(memory_space=pltpu.HBM)
    operands = [
        pltpu.with_memory_space_constraint(x, pltpu.HBM if i in far else pltpu.VMEM)
        for i, x in enumerate(operands)
    ]
    return pl.pallas_call(
        body,
        out_shape=out_shape,
        in_specs=[hbm if i in far else near for i in range(len(operands))],
        out_specs=jax.tree.map(lambda _: near, out_shape),
        scratch_shapes=scratch,
        compiler_params=pltpu.CompilerParams(vmem_limit_bytes=limit * 1024 * 1024),
        name=name,
    )(*operands)


def vmem(shape, dtype):
    return pltpu.VMEM(shape, dtype)


def gelu_twice(x):
    inner = x * (math.sqrt(2.0 / math.pi) + (math.sqrt(2.0 / math.pi) * 0.044715) * (x * x))
    return x + x * jnp.tanh(inner)


def nt_dot(a, b):
    return lax.dot_general(a, b, (((1,), (1,)), ((), ())), preferred_element_type=f32)


def mm(a, b):
    return jnp.dot(a, b, preferred_element_type=f32)


def cost_of(sources_ref, window, out_ref, start):
    groups, count, depth = sources_ref.shape
    every = sources_ref[...].reshape(groups * count, depth)
    for n in range(0, window.shape[0], 256):
        value = nt_dot(every, window[n : n + 256]) * (1.0 / math.sqrt(depth))
        out_ref[:, :, start + n : start + n + 256] = value.astype(bf16).reshape(groups, count, 256)


def own_body(rows_ref, sources_ref, out_ref):
    parts = []
    for z in range(rows_ref.shape[0]):
        for half in (slice(0, 32), slice(32, 64)):
            parts += [rows_ref[z, 0, half], rows_ref[z, 1, half]]
    cost_of(sources_ref, jnp.concatenate(parts, axis=0), out_ref, 0)


def halo_body(left_ref, right_ref, sources_ref, own_ref, out_ref):
    out_ref[:, :, :OWN] = own_ref[...]
    parts = []
    for z in range(left_ref.shape[0]):
        for r in range(2):
            parts += [left_ref[z, r], right_ref[z, r]]
    cost_of(sources_ref, jnp.concatenate(parts, axis=0), out_ref, OWN)


def cost_maps(rows, left, right, sources):
    own = call(own_body, vmem(sources.shape[:2] + (OWN,), bf16), (rows, sources), "own_columns", 16)
    shape = vmem(sources.shape[:2] + (OWN + OWN // 2,), bf16)
    return call(halo_body, shape, (left, right, sources, own), "halo_columns", 16)


def band(taps, out_ref, step, block):
    depth = taps.shape[0] // 6
    rows = out_ref.shape[0] // 6
    for t in range(taps.shape[1] // 128):
        lane = lax.broadcasted_iota(jnp.int32, (depth, 128), 1) // block
        for kh in range(6):
            tile = taps[depth * kh : depth * (kh + 1), 128 * t : 128 * (t + 1)]
            total = jnp.zeros((rows, 128), f32)
            for b in range(128 // block):
                top = step * (b + t * (128 // block))
                piece = [jnp.where(lane == b, 0.5 * tile, 0.0)]
                if top:
                    piece = [jnp.zeros((top, 128), f32)] + piece
                if rows - top - depth:
                    piece = piece + [jnp.zeros((rows - top - depth, 128), f32)]
                total = total + jnp.concatenate(piece, axis=0)
            out_ref[kh * rows : (kh + 1) * rows, 128 * t : 128 * (t + 1)] = total.astype(bf16)


def repeated(kernel_ref):
    width = kernel_ref.shape[1]
    row = lax.broadcasted_iota(jnp.int32, (width, 256), 0)
    lane = lax.broadcasted_iota(jnp.int32, (width, 256), 1)
    pick = jnp.where(lane % width == row, 1.0, 0.0).astype(bf16)
    return mm(kernel_ref[...], pick)


def band_body(
    one_ref,
    two_ref,
    three_ref,
    latents_ref,
    key_ref,
    pos_key_ref,
    out_one,
    out_two,
    out_three,
    out_query,
    out_pos,
):
    row = lax.broadcasted_iota(jnp.int32, (128, 256), 0)
    place = lax.broadcasted_iota(jnp.int32, (128, 256), 1) // 16
    odd = (row // 32) % 2 == 1
    x = row % 32
    upper = row >= 64
    halo = jnp.where(x < 16, x - 16, x + 48)
    columns = (
        jnp.where(upper, halo, x),
        jnp.where(upper, x + 32, x),
        jnp.where(upper, x + 32, halo),
    )
    one = repeated(one_ref)
    for n in range(3):
        tap = columns[n] + 14 - 2 * (place + 16 * n)
        for j in range(3):
            total = jnp.zeros((128, 256), f32)
            for kw in range(6):
                first = one[12 * j + kw : 12 * j + kw + 1]
                second = one[12 * j + 6 + kw : 12 * j + 7 + kw]
                total = jnp.where(tap == kw, jnp.where(odd, second, first), total)
            out_one[128 * j : 128 * (j + 1), 256 * n : 256 * (n + 1)] = total.astype(bf16)
    band(repeated(two_ref), out_two, 32, 32)
    band(repeated(three_ref), out_three, 64, 64)

    def exact_nt(a, b):
        return lax.dot_general(
            a, b, (((1,), (1,)), ((), ())), precision=exact, preferred_element_type=f32
        )

    latents = jnp.concatenate([latents_ref[...]] * 16, axis=0)
    query = exact_nt(key_ref[...], latents)
    patch = lax.broadcasted_iota(jnp.int32, (64, 128), 1) // 8 % 8
    for w in range(8):
        out_query[64 * w : 64 * (w + 1), :] = jnp.where(patch == w, query, 0.0).astype(bf16)
    pos = exact_nt(pos_key_ref[...].reshape(128, 128), latents)
    row = lax.broadcasted_iota(jnp.int32, (128, 128), 0)
    patch = lax.broadcasted_iota(jnp.int32, (128, 128), 1) // 8
    pos = jnp.where(patch % 8 == row % 8, pos, 0.0)
    out_pos[...] = jnp.sum(pos.reshape(16, 8, 128), axis=1)


def bands(kernel_one, kernel_two, kernel_three, latents, w_key, pos_key):
    shapes = (
        jax.ShapeDtypeStruct((384, 768), bf16),
        jax.ShapeDtypeStruct((2304, 256), bf16),
        jax.ShapeDtypeStruct((2304, 256), bf16),
        jax.ShapeDtypeStruct((512, 128), bf16),
        jax.ShapeDtypeStruct((16, 128), f32),
    )
    kernels = (
        kernel_one.reshape(36, 16),
        kernel_two.reshape(6 * 96, 32),
        kernel_three.reshape(6 * 192, 64),
    )
    return call(band_body, shapes, kernels + (latents, w_key, pos_key), "bands", 16)


def encode_body(
    cost_ref,
    one_far,
    two_far,
    three_far,
    query_ref,
    pos_ref,
    bias_one,
    bias_two,
    bias_three,
    spread_far,
    out_ref,
    pairs,
    hidden_one,
    hidden_two,
    features,
    score_ref,
    one_ref,
    two_ref,
    three_ref,
    spread_ref,
    arrived,
):
    count = cost_ref.shape[1]
    fetches = [
        pltpu.make_async_copy(far, near, arrived.at[i])
        for i, (far, near) in enumerate(
            (
                (one_far, one_ref),
                (two_far, two_ref),
                (three_far, three_ref),
                (spread_far, spread_ref),
            )
        )
    ]
    for fetch in fetches:
        fetch.start()
    blank = jnp.zeros((EDGE, count, 384), bf16)
    pairs[0:EDGE] = blank
    pairs[EDGE + PAIRS : 2 * EDGE + PAIRS] = blank

    def place(i, _):
        for z in range(4):
            own = cost_ref[i, :, 128 * z : 128 * (z + 1)]
            halo = cost_ref[i, :, OWN + 64 * z : OWN + 64 * (z + 1)]
            pairs[EDGE + z * GROUP + i] = jnp.concatenate(
                [own[:, :64], halo, own, halo, own[:, 64:]], axis=1
            )
        return 0

    lax.fori_loop(0, GROUP, place, 0, unroll=2)

    def first(i, _):
        step = ROWS_ONE
        h = i * step
        for n in range(3):
            lanes = slice(128 * n, 128 * (n + 1))
            left = jnp.concatenate(
                [pairs[pl.ds(h + j, step), :, lanes].reshape(step * count, 128) for j in range(3)],
                axis=1,
            )
            lanes = slice(256 * n, 256 * (n + 1))
            value = gelu_twice(mm(left, one_ref[:, lanes]) + bias_one[:, lanes])
            hidden_one[pl.ds(i * (step // 2), step // 2), :, :, lanes] = value.astype(bf16).reshape(
                step // 2, 2, count, 256
            )
        return 0

    fetches[0].wait()
    lax.fori_loop(0, pl.cdiv(76, ROWS_ONE), first, 0)
    fetches[1].wait()

    def taps(source, h, step, lanes):
        parts = [
            source[pl.ds(h + k // 2, step), k % 2, :, lanes].reshape(step * count, -1)
            for k in range(6)
        ]
        return jnp.concatenate(parts, axis=1)

    short = jnp.concatenate([two_ref[384 * k : 384 * k + 256, :128] for k in range(6)], axis=0)

    def second(i, _):
        step = ROWS_TWO
        h = i * step
        for n in range(3):
            lanes = slice(256 * n, min(256 * n + 384, 768))
            right, bias = (two_ref[...], bias_two[...])
            if n == 2:
                right, bias = (short, bias_two[:, :128])
            value = gelu_twice(mm(taps(hidden_one, h, step, lanes), right) + bias)
            lanes = slice(256 * n, 256 * n + value.shape[1])
            hidden_two[pl.ds(i * (step // 2), step // 2), :, :, lanes] = value.astype(bf16).reshape(
                step // 2, 2, count, -1
            )
        return 0

    lax.fori_loop(0, 36 // ROWS_TWO, second, 0)

    def third(i, _):
        step = ROWS_THREE
        h = i * step
        for n in range(2):
            left = taps(hidden_two, h, step, slice(256 * n, 256 * n + 384))
            value = mm(left, three_ref[...]) + bias_three[...]
            features[pl.ds(h, step), :, 256 * n : 256 * (n + 1)] = value.astype(bf16).reshape(
                step, count, 256
            )
        return 0

    fetches[2].wait()
    lax.fori_loop(0, 16 // ROWS_THREE, third, 0)
    fetches[3].wait()

    scale = 1.0 / math.sqrt(128)

    value = mm(features[...].reshape(16 * count, 512), query_ref[...]).reshape(16, count, 128)
    value = (value + pos_ref[...][:, None, :]) * scale
    score_ref[...] = value
    peak = jnp.max(value, axis=0)
    for k in (8, 16, 32):
        peak = jnp.maximum(peak, pltpu.roll(peak, k, 1))
    low = lax.broadcasted_iota(jnp.int32, (count, 128), 1) < 64

    value = jnp.exp(score_ref[...] - peak)
    total = jnp.sum(value, axis=0)
    head = value.astype(bf16).astype(f32)
    shares = jnp.where(low, head, value - head).astype(bf16).reshape(16 * count, 128)
    for k in (8, 16, 32):
        total = total + pltpu.roll(total, k, 1)

    def gather(latent):
        spread = spread_ref[:, 512 * latent : 512 * (latent + 1)]

        value = mm(shares, spread).reshape(16, count, 512)
        acc = jnp.sum(value * features[...].astype(f32), axis=0)
        acc = (acc[:, :128] + acc[:, 128:256]) + (acc[:, 256:384] + acc[:, 384:])
        return acc + pltpu.roll(acc, 64, 1)

    for k in range(4):
        out_ref[:, 128 * k : 128 * (k + 1)] = jnp.where(low, gather(2 * k), gather(2 * k + 1))
    out_ref[:, 512:] = jnp.where(low, peak, total)


def encode(cost, prepared, biases, spread):
    count = cost.shape[1]
    scratch = [
        vmem((pl.cdiv(76, ROWS_ONE) * ROWS_ONE + 2, count, 384), bf16),
        vmem((pl.cdiv(76, ROWS_ONE) * (ROWS_ONE // 2), 2, count, 768), bf16),
        vmem((18, 2, count, 640), bf16),
        vmem((16, count, 512), bf16),
        vmem((16, count, 128), f32),
        vmem((384, 768), bf16),
        vmem((2304, 256), bf16),
        vmem((2304, 256), bf16),
        vmem((128, 4096), bf16),
        pltpu.SemaphoreType.DMA((4,)),
    ]
    operands = (cost, *prepared, *biases, spread)
    shape = vmem((count, 640), f32)
    return call(encode_body, shape, operands, "encode", 40, scratch, far=(1, 2, 3, 9))


def combine_body(parts_ref, spread_ref, out_ref):
    tiles, count, _ = parts_ref.shape
    low = lax.broadcasted_iota(jnp.int32, (count, 128), 1) < 64
    stats = [parts_ref[t, :, 512:] for t in range(tiles)]
    peak = functools.reduce(jnp.maximum, stats)
    factors = [jnp.where(low, jnp.exp(stat - peak), 0.0) for stat in stats]
    totals = [factor * pltpu.roll(stat, 64, 1) for factor, stat in zip(factors, stats)]
    total = jnp.where(low, functools.reduce(jnp.add, totals), 1.0)
    shares = jnp.concatenate([factor / total for factor in factors], axis=0)
    wide = jnp.dot(shares, spread_ref[...], precision=exact, preferred_element_type=f32)
    attended = jnp.zeros((count, 512), f32)
    for t in range(tiles):
        attended = attended + wide[count * t : count * (t + 1)] * parts_ref[t, :, :512]
    for t in range(tiles):
        out_ref[t] = attended


def combine(parts, spread):
    return call(
        combine_body, vmem(parts.shape[:2] + (512,), f32), (parts, spread), "combine", 8
    )


def value_body(attended_ref, value_ref, out_ref):
    count = attended_ref.shape[0]
    low = lax.broadcasted_iota(jnp.int32, (count, 128), 1) < 64
    parts = []
    for latent in range(8):
        part = attended_ref[:, 128 * (latent // 2) : 128 * (latent // 2 + 1)]
        parts.append(jnp.where(low == (latent % 2 == 0), part, 0.0))
    value = jnp.dot(
        jnp.concatenate(parts, axis=0),
        value_ref[...],
        precision=exact,
        preferred_element_type=f32,
    )
    for latent in range(8):
        out_ref[:, latent, :] = value[count * latent : count * (latent + 1)]


def valued(attended, value_weight):
    shape = jax.ShapeDtypeStruct((attended.shape[0], 8, 128), f32)
    return call(value_body, shape, (attended, value_weight), "valued", 8)


def prepare(
    kernel_one, kernel_two, kernel_three, latents, pos_key, first_conv_bias, shift_two, shift_three, w_key
):
    prepared = bands(kernel_one, kernel_two, kernel_three, latents, w_key, pos_key)
    lane = np.arange(128)[:, None] % 64
    column = np.arange(8 * 512)[None, :]
    spread = jnp.asarray((lane == (column % 512) // 64 * 8 + column // 512).astype(bf16))
    biases = (
        jnp.tile(first_conv_bias, 48)[None],
        jnp.tile(shift_two, 8)[None],
        jnp.tile(shift_three, 4)[None],
    )
    return prepared, biases, spread


def on_device(
    target,
    sources,
    kernel_one,
    first_conv_bias,
    kernel_two,
    shift_two,
    kernel_three,
    shift_three,
    latents,
    pos_key,
    w_key,
    value_weight,
):
    tiles = lax.axis_size("tile")
    groups = lax.axis_size("xy")
    copies = jnp.broadcast_to(sources[None], (groups,) + sources.shape)
    copies, target = lax.optimization_barrier((copies, target))
    every = lax.all_to_all(copies, "xy", 0, 0)
    rows = lax.all_gather(target, "zh", axis=0)
    width = rows.shape[2]
    up = [(i, i + 1) for i in range(tiles - 1)]
    down = [(j, i) for i, j in up]
    left = lax.ppermute(rows[:, :, width - HALO :], "tile", up)
    right = lax.ppermute(rows[:, :, :HALO], "tile", down)
    cost = cost_maps(rows, left, right, every)
    weights = (kernel_one, kernel_two, kernel_three, latents, pos_key)
    cost, weights, value_weight = lax.optimization_barrier((cost, weights, value_weight))
    value_weight = jnp.concatenate([value_weight, value_weight], axis=0)
    prepared = prepare(*weights, first_conv_bias, shift_two, shift_three, w_key)
    parts = encode(lax.all_to_all(cost, "xy", 0, 0), *prepared)
    parts, value_weight = lax.optimization_barrier((parts, value_weight))
    parts = lax.all_to_all(parts.reshape(tiles, -1, parts.shape[1]), "tile", 0, 0)
    latent = np.arange(128)[:, None]
    spread = jnp.asarray((latent == np.arange(512)[None, :] // 64).astype(np.float32))
    attended = lax.all_to_all(combine(parts, spread), "tile", 0, 0)
    return valued(attended.reshape(-1, attended.shape[-1]), value_weight)


def solution(mesh):
    src, tile = mesh.devices.shape
    split = Mesh(mesh.devices.reshape(src // GROUP, GROUP, tile), ("zh", "xy", "tile"))
    rows = ("zh", "xy")
    return jax.shard_map(
        on_device,
        mesh=split,
        in_specs=(
            P(rows, "tile", None),
            P(rows, None),
            P(),
            P(),
            P(),
            P(),
            P(),
            P(),
            P(),
            P(None, "tile", None),
            P(),
            P(),
        ),
        out_specs=P(rows, None, None),
        check_vma=False,
    )
```

```python
import functools
import math

import jax
import jax.numpy as jnp
import numpy as np
from jax import lax
from jax.experimental import pallas as pl
from jax.experimental.pallas import tpu as pltpu
from jax.sharding import Mesh, PartitionSpec as P

exact = lax.Precision.HIGHEST
f32 = jnp.float32
bf16 = jnp.bfloat16

GROUP = 16
HALO = 16
OWN = 512
PAIRS = 64
EDGE = 7
ROWS_ONE = 38
ROWS_TWO = 18
ROWS_THREE = 16


def call(body, out_shape, operands, name, limit, scratch=(), far=()):
    near = pl.BlockSpec(memory_space=pltpu.VMEM)
    hbm = pl.BlockSpec(memory_space=pltpu.HBM)
    operands = [
        pltpu.with_memory_space_constraint(x, pltpu.HBM if i in far else pltpu.VMEM)
        for i, x in enumerate(operands)
    ]
    return pl.pallas_call(
        body,
        out_shape=out_shape,
        in_specs=[hbm if i in far else near for i in range(len(operands))],
        out_specs=jax.tree.map(lambda _: near, out_shape),
        scratch_shapes=scratch,
        compiler_params=pltpu.CompilerParams(vmem_limit_bytes=limit * 1024 * 1024),
        name=name,
    )(*operands)


def vmem(shape, dtype):
    return pltpu.VMEM(shape, dtype)


def gelu_twice(x):
    inner = x * (math.sqrt(2.0 / math.pi) + (math.sqrt(2.0 / math.pi) * 0.044715) * (x * x))
    return x + x * jnp.tanh(inner)


def nt_dot(a, b):
    return lax.dot_general(a, b, (((1,), (1,)), ((), ())), preferred_element_type=f32)


def mm(a, b):
    return jnp.dot(a, b, preferred_element_type=f32)


def cost_of(sources_ref, window, out_ref, start):
    groups, count, depth = sources_ref.shape
    every = sources_ref[...].reshape(groups * count, depth)
    for n in range(0, window.shape[0], 256):
        value = nt_dot(every, window[n : n + 256]) * (1.0 / math.sqrt(depth))
        out_ref[:, :, start + n : start + n + 256] = value.astype(bf16).reshape(groups, count, 256)


def own_body(rows_ref, sources_ref, out_ref):
    parts = []
    for z in range(rows_ref.shape[0]):
        for half in (slice(0, 32), slice(32, 64)):
            parts += [rows_ref[z, 0, half], rows_ref[z, 1, half]]
    cost_of(sources_ref, jnp.concatenate(parts, axis=0), out_ref, 0)


def halo_body(left_ref, right_ref, sources_ref, _, out_ref, near, sent):
    parts = []
    for z in range(left_ref.shape[0]):
        for r in range(2):
            parts += [left_ref[z, r], right_ref[z, r]]
    cost_of(sources_ref, jnp.concatenate(parts, axis=0), near, 0)
    store = pltpu.make_async_copy(near, out_ref.at[:, :, pl.ds(OWN, OWN // 2)], sent)
    store.start()
    store.wait()


def cost_maps(rows, left, right, sources):
    shape = jax.ShapeDtypeStruct(sources.shape[:2] + (OWN + OWN // 2,), bf16)
    own = call(own_body, shape, (rows, sources), "own_columns", 16)
    near = pl.BlockSpec(memory_space=pltpu.VMEM)
    hbm = pl.BlockSpec(memory_space=pltpu.HBM)
    operands = [pltpu.with_memory_space_constraint(x, pltpu.VMEM) for x in (left, right, sources)]
    return pl.pallas_call(
        halo_body,
        out_shape=shape,
        in_specs=[near, near, near, hbm],
        out_specs=hbm,
        scratch_shapes=[
            vmem(sources.shape[:2] + (OWN // 2,), bf16),
            pltpu.SemaphoreType.DMA(()),
        ],
        input_output_aliases={3: 0},
        compiler_params=pltpu.CompilerParams(vmem_limit_bytes=16 * 1024 * 1024),
        name="halo_columns",
    )(*operands, pltpu.with_memory_space_constraint(own, pltpu.HBM))


def band(taps, out_ref, step, block):
    depth = taps.shape[0] // 6
    rows = out_ref.shape[0] // 6
    for t in range(taps.shape[1] // 128):
        lane = lax.broadcasted_iota(jnp.int32, (depth, 128), 1) // block
        for kh in range(6):
            tile = taps[depth * kh : depth * (kh + 1), 128 * t : 128 * (t + 1)]
            total = jnp.zeros((rows, 128), f32)
            for b in range(128 // block):
                top = step * (b + t * (128 // block))
                piece = [jnp.where(lane == b, 0.5 * tile, 0.0)]
                if top:
                    piece = [jnp.zeros((top, 128), f32)] + piece
                if rows - top - depth:
                    piece = piece + [jnp.zeros((rows - top - depth, 128), f32)]
                total = total + jnp.concatenate(piece, axis=0)
            out_ref[kh * rows : (kh + 1) * rows, 128 * t : 128 * (t + 1)] = total.astype(bf16)


def repeated(kernel_ref):
    width = kernel_ref.shape[1]
    row = lax.broadcasted_iota(jnp.int32, (width, 256), 0)
    lane = lax.broadcasted_iota(jnp.int32, (width, 256), 1)
    pick = jnp.where(lane % width == row, 1.0, 0.0).astype(bf16)
    return mm(kernel_ref[...], pick)


def band_body(
    one_ref,
    two_ref,
    three_ref,
    latents_ref,
    key_ref,
    pos_key_ref,
    out_one,
    out_two,
    out_three,
    out_query,
    out_pos,
):
    row = lax.broadcasted_iota(jnp.int32, (128, 256), 0)
    place = lax.broadcasted_iota(jnp.int32, (128, 256), 1) // 16
    odd = (row // 32) % 2 == 1
    x = row % 32
    upper = row >= 64
    halo = jnp.where(x < 16, x - 16, x + 48)
    columns = (
        jnp.where(upper, halo, x),
        jnp.where(upper, x + 32, x),
        jnp.where(upper, x + 32, halo),
    )
    one = repeated(one_ref)
    for n in range(3):
        tap = columns[n] + 14 - 2 * (place + 16 * n)
        for j in range(3):
            total = jnp.zeros((128, 256), f32)
            for kw in range(6):
                first = one[12 * j + kw : 12 * j + kw + 1]
                second = one[12 * j + 6 + kw : 12 * j + 7 + kw]
                total = jnp.where(tap == kw, jnp.where(odd, second, first), total)
            out_one[128 * j : 128 * (j + 1), 256 * n : 256 * (n + 1)] = total.astype(bf16)
    band(repeated(two_ref), out_two, 32, 32)
    band(repeated(three_ref), out_three, 64, 64)

    def exact_nt(a, b):
        return lax.dot_general(
            a, b, (((1,), (1,)), ((), ())), precision=exact, preferred_element_type=f32
        )

    latents = jnp.concatenate([latents_ref[...]] * 16, axis=0)
    query = exact_nt(key_ref[...], latents)
    patch = lax.broadcasted_iota(jnp.int32, (64, 128), 1) // 8 % 8
    for w in range(8):
        out_query[64 * w : 64 * (w + 1), :] = jnp.where(patch == w, query, 0.0).astype(bf16)
    pos = exact_nt(pos_key_ref[...].reshape(128, 128), latents)
    row = lax.broadcasted_iota(jnp.int32, (128, 128), 0)
    patch = lax.broadcasted_iota(jnp.int32, (128, 128), 1) // 8
    pos = jnp.where(patch % 8 == row % 8, pos, 0.0)
    out_pos[...] = jnp.sum(pos.reshape(16, 8, 128), axis=1)


def bands(kernel_one, kernel_two, kernel_three, latents, w_key, pos_key):
    shapes = (
        jax.ShapeDtypeStruct((384, 768), bf16),
        jax.ShapeDtypeStruct((2304, 256), bf16),
        jax.ShapeDtypeStruct((2304, 256), bf16),
        jax.ShapeDtypeStruct((512, 128), bf16),
        jax.ShapeDtypeStruct((16, 128), f32),
    )
    kernels = (
        kernel_one.reshape(36, 16),
        kernel_two.reshape(6 * 96, 32),
        kernel_three.reshape(6 * 192, 64),
    )
    return call(band_body, shapes, kernels + (latents, w_key, pos_key), "bands", 16)


def encode_body(
    cost_ref,
    one_far,
    two_far,
    three_far,
    query_ref,
    pos_ref,
    bias_one,
    bias_two,
    bias_three,
    spread_far,
    out_ref,
    pairs,
    hidden_one,
    hidden_two,
    features,
    score_ref,
    one_ref,
    two_ref,
    three_ref,
    spread_ref,
    arrived,
):
    count = cost_ref.shape[1]
    fetches = [
        pltpu.make_async_copy(far, near, arrived.at[i])
        for i, (far, near) in enumerate(
            (
                (one_far, one_ref),
                (two_far, two_ref),
                (three_far, three_ref),
                (spread_far, spread_ref),
            )
        )
    ]
    for fetch in fetches:
        fetch.start()
    blank = jnp.zeros((EDGE, count, 384), bf16)
    pairs[0:EDGE] = blank
    pairs[EDGE + PAIRS : 2 * EDGE + PAIRS] = blank

    def place(i, _):
        for z in range(4):
            own = cost_ref[i, :, 128 * z : 128 * (z + 1)]
            halo = cost_ref[i, :, OWN + 64 * z : OWN + 64 * (z + 1)]
            pairs[EDGE + z * GROUP + i] = jnp.concatenate(
                [own[:, :64], halo, own, halo, own[:, 64:]], axis=1
            )
        return 0

    lax.fori_loop(0, GROUP, place, 0, unroll=2)

    def first(i, _):
        step = ROWS_ONE
        h = i * step
        for n in range(3):
            lanes = slice(128 * n, 128 * (n + 1))
            left = jnp.concatenate(
                [pairs[pl.ds(h + j, step), :, lanes].reshape(step * count, 128) for j in range(3)],
                axis=1,
            )
            lanes = slice(256 * n, 256 * (n + 1))
            value = gelu_twice(mm(left, one_ref[:, lanes]) + bias_one[:, lanes])
            hidden_one[pl.ds(i * (step // 2), step // 2), :, :, lanes] = value.astype(bf16).reshape(
                step // 2, 2, count, 256
            )
        return 0

    fetches[0].wait()
    lax.fori_loop(0, pl.cdiv(76, ROWS_ONE), first, 0)
    fetches[1].wait()

    def taps(source, h, step, lanes):
        parts = [
            source[pl.ds(h + k // 2, step), k % 2, :, lanes].reshape(step * count, -1)
            for k in range(6)
        ]
        return jnp.concatenate(parts, axis=1)

    short = jnp.concatenate([two_ref[384 * k : 384 * k + 256, :128] for k in range(6)], axis=0)

    def second(i, _):
        step = ROWS_TWO
        h = i * step
        for n in range(3):
            lanes = slice(256 * n, min(256 * n + 384, 768))
            right, bias = (two_ref[...], bias_two[...])
            if n == 2:
                right, bias = (short, bias_two[:, :128])
            value = gelu_twice(mm(taps(hidden_one, h, step, lanes), right) + bias)
            lanes = slice(256 * n, 256 * n + value.shape[1])
            hidden_two[pl.ds(i * (step // 2), step // 2), :, :, lanes] = value.astype(bf16).reshape(
                step // 2, 2, count, -1
            )
        return 0

    lax.fori_loop(0, 36 // ROWS_TWO, second, 0)

    def third(i, _):
        step = ROWS_THREE
        h = i * step
        for n in range(2):
            left = taps(hidden_two, h, step, slice(256 * n, 256 * n + 384))
            value = mm(left, three_ref[...]) + bias_three[...]
            features[pl.ds(h, step), :, 256 * n : 256 * (n + 1)] = value.astype(bf16).reshape(
                step, count, 256
            )
        return 0

    fetches[2].wait()
    lax.fori_loop(0, 16 // ROWS_THREE, third, 0)
    fetches[3].wait()

    scale = 1.0 / math.sqrt(128)

    value = mm(features[...].reshape(16 * count, 512), query_ref[...]).reshape(16, count, 128)
    value = (value + pos_ref[...][:, None, :]) * scale
    score_ref[...] = value
    peak = jnp.max(value, axis=0)
    for k in (8, 16, 32):
        peak = jnp.maximum(peak, pltpu.roll(peak, k, 1))
    low = lax.broadcasted_iota(jnp.int32, (count, 128), 1) < 64

    value = jnp.exp(score_ref[...] - peak)
    total = jnp.sum(value, axis=0)
    head = value.astype(bf16).astype(f32)
    shares = jnp.where(low, head, value - head).astype(bf16).reshape(16 * count, 128)
    for k in (8, 16, 32):
        total = total + pltpu.roll(total, k, 1)

    def gather(latent):
        spread = spread_ref[:, 512 * latent : 512 * (latent + 1)]

        value = mm(shares, spread).reshape(16, count, 512)
        acc = jnp.sum(value * features[...].astype(f32), axis=0)
        acc = (acc[:, :128] + acc[:, 128:256]) + (acc[:, 256:384] + acc[:, 384:])
        return acc + pltpu.roll(acc, 64, 1)

    for k in range(4):
        out_ref[:, 128 * k : 128 * (k + 1)] = jnp.where(low, gather(2 * k), gather(2 * k + 1))
    out_ref[:, 512:] = jnp.where(low, peak, total)


def encode(cost, prepared, biases, spread):
    count = cost.shape[1]
    scratch = [
        vmem((pl.cdiv(76, ROWS_ONE) * ROWS_ONE + 2, count, 384), bf16),
        vmem((pl.cdiv(76, ROWS_ONE) * (ROWS_ONE // 2), 2, count, 768), bf16),
        vmem((18, 2, count, 640), bf16),
        vmem((16, count, 512), bf16),
        vmem((16, count, 128), f32),
        vmem((384, 768), bf16),
        vmem((2304, 256), bf16),
        vmem((2304, 256), bf16),
        vmem((128, 4096), bf16),
        pltpu.SemaphoreType.DMA((4,)),
    ]
    operands = (cost, *prepared, *biases, spread)
    shape = vmem((count, 640), f32)
    return call(encode_body, shape, operands, "encode", 40, scratch, far=(1, 2, 3, 9))


def combine_body(parts_ref, spread_ref, out_ref):
    tiles, count, _ = parts_ref.shape
    low = lax.broadcasted_iota(jnp.int32, (count, 128), 1) < 64
    stats = [parts_ref[t, :, 512:] for t in range(tiles)]
    peak = functools.reduce(jnp.maximum, stats)
    factors = [jnp.where(low, jnp.exp(stat - peak), 0.0) for stat in stats]
    totals = [factor * pltpu.roll(stat, 64, 1) for factor, stat in zip(factors, stats)]
    total = jnp.where(low, functools.reduce(jnp.add, totals), 1.0)
    shares = jnp.concatenate([factor / total for factor in factors], axis=0)
    wide = jnp.dot(shares, spread_ref[...], precision=exact, preferred_element_type=f32)
    attended = jnp.zeros((count, 512), f32)
    for t in range(tiles):
        attended = attended + wide[count * t : count * (t + 1)] * parts_ref[t, :, :512]
    for t in range(tiles):
        out_ref[t] = attended


def combine(parts, spread):
    return call(
        combine_body, vmem(parts.shape[:2] + (512,), f32), (parts, spread), "combine", 8
    )


def value_body(attended_ref, value_ref, out_ref):
    count = attended_ref.shape[0]
    low = lax.broadcasted_iota(jnp.int32, (count, 128), 1) < 64
    parts = []
    for latent in range(8):
        part = attended_ref[:, 128 * (latent // 2) : 128 * (latent // 2 + 1)]
        parts.append(jnp.where(low == (latent % 2 == 0), part, 0.0))
    value = jnp.dot(
        jnp.concatenate(parts, axis=0),
        value_ref[...],
        precision=exact,
        preferred_element_type=f32,
    )
    for latent in range(8):
        out_ref[:, latent, :] = value[count * latent : count * (latent + 1)]


def valued(attended, value_weight):
    shape = jax.ShapeDtypeStruct((attended.shape[0], 8, 128), f32)
    return call(value_body, shape, (attended, value_weight), "valued", 8)


def prepare(
    kernel_one, kernel_two, kernel_three, latents, pos_key, first_conv_bias, shift_two, shift_three, w_key
):
    prepared = bands(kernel_one, kernel_two, kernel_three, latents, w_key, pos_key)
    lane = np.arange(128)[:, None] % 64
    column = np.arange(8 * 512)[None, :]
    spread = jnp.asarray((lane == (column % 512) // 64 * 8 + column // 512).astype(bf16))
    biases = (
        jnp.tile(first_conv_bias, 48)[None],
        jnp.tile(shift_two, 8)[None],
        jnp.tile(shift_three, 4)[None],
    )
    return prepared, biases, spread


def on_device(
    target,
    sources,
    kernel_one,
    first_conv_bias,
    kernel_two,
    shift_two,
    kernel_three,
    shift_three,
    latents,
    pos_key,
    w_key,
    value_weight,
):
    tiles = lax.axis_size("tile")
    groups = lax.axis_size("xy")
    copies = jnp.broadcast_to(sources[None], (groups,) + sources.shape)
    copies, target = lax.optimization_barrier((copies, target))
    every = lax.all_to_all(copies, "xy", 0, 0)
    rows = lax.all_gather(target, "zh", axis=0)
    width = rows.shape[2]
    up = [(i, i + 1) for i in range(tiles - 1)]
    down = [(j, i) for i, j in up]
    left = lax.ppermute(rows[:, :, width - HALO :], "tile", up)
    right = lax.ppermute(rows[:, :, :HALO], "tile", down)
    cost = cost_maps(rows, left, right, every)
    weights = (kernel_one, kernel_two, kernel_three, latents, pos_key)
    cost, weights, value_weight = lax.optimization_barrier((cost, weights, value_weight))
    value_weight = jnp.concatenate([value_weight, value_weight], axis=0)
    prepared = prepare(*weights, first_conv_bias, shift_two, shift_three, w_key)
    parts = encode(lax.all_to_all(cost, "xy", 0, 0), *prepared)
    parts, value_weight = lax.optimization_barrier((parts, value_weight))
    parts = lax.all_to_all(parts.reshape(tiles, -1, parts.shape[1]), "tile", 0, 0)
    latent = np.arange(128)[:, None]
    spread = jnp.asarray((latent == np.arange(512)[None, :] // 64).astype(np.float32))
    attended = lax.all_to_all(combine(parts, spread), "tile", 0, 0)
    return valued(attended.reshape(-1, attended.shape[-1]), value_weight)


def solution(mesh):
    src, tile = mesh.devices.shape
    split = Mesh(mesh.devices.reshape(src // GROUP, GROUP, tile), ("zh", "xy", "tile"))
    rows = ("zh", "xy")
    return jax.shard_map(
        on_device,
        mesh=split,
        in_specs=(
            P(rows, "tile", None),
            P(rows, None),
            P(),
            P(),
            P(),
            P(),
            P(),
            P(),
            P(),
            P(None, "tile", None),
            P(),
            P(),
        ),
        out_specs=P(rows, None, None),
        check_vma=False,
    )
```
